32 devices in a mesh: dp: 8 (over z, x), group: 4 (over y, core).
Axes of the slice: x: 2, y: 2, z: 4, core: 2. Of those that a mesh axis runs over, the one named last changes fastest.
Arguments:
- tokens: bfloat16 [4096, 960], P(('dp', 'group')), may hold values from -6 to 6
- cotangent: bfloat16 [4096, 960], P(('dp', 'group')), may hold values from -6 to 6
- prenorm_master: float32 [960], P('group'), may hold values from 0.5 to 1.5
- query_master: float32 [960, 960], P('group', 'dp'), may hold values from -0.1875 to 0.1875
- key_master_copy: float32 [960, 320], P('group', 'dp'), may hold values from -0.1875 to 0.1875
- value_master_copy: float32 [960, 320], P('group', 'dp'), may hold values from -0.1875 to 0.1875
- out_master: float32 [960, 960], P('group', 'dp'), may hold values from -0.75 to 0.75
- midnorm_master: float32 [960], P('group'), may hold values from 0.5 to 1.5
- gate_master: float32 [960, 2560], P('group', 'dp'), may hold values from -0.1875 to 0.1875
- up_master: float32 [960, 2560], P('group', 'dp'), may hold values from -0.1875 to 0.1875
- down_master: float32 [2560, 960], P('group', 'dp'), may hold values from -0.125 to 0.125
- prenorm_mean: float32 [960], P('group'), may hold values from -103.68 to 103.68
- query_mean: float32 [960, 960], P('group', 'dp'), may hold values from -80.64 to 80.64
- key_first_moment: float32 [960, 320], P('group', 'dp'), may hold values from -111.36 to 111.36
- value_first_moment: float32 [960, 320], P('group', 'dp'), may hold values from -119.04 to 119.04
- out_mean: float32 [960, 960], P('group', 'dp'), may hold values from -19.968 to 19.968
- midnorm_mean: float32 [960], P('group'), may hold values from -46.08 to 46.08
- gate_mean: float32 [960, 2560], P('group', 'dp'), may hold values from -20.736 to 20.736
- up_mean: float32 [960, 2560], P('group', 'dp'), may hold values from -32.256 to 32.256
- down_mean: float32 [2560, 960], P('group', 'dp'), may hold values from -44.16 to 44.16
- prenorm_square: float32 [960], P('group'), may hold values from 307.2 to 1228.8
- query_square: float32 [960, 960], P('group', 'dp'), may hold values from 184.32 to 737.28
- key_second_moment: float32 [960, 320], P('group', 'dp'), may hold values from 368.64 to 1474.56
- value_second_moment: float32 [960, 320], P('group', 'dp'), may hold values from 409.6 to 1638.4
- out_square: float32 [960, 960], P('group', 'dp'), may hold values from 12.288 to 49.152
- midnorm_square: float32 [960], P('group'), may hold values from 61.44 to 245.76
- gate_square: float32 [960, 2560], P('group', 'dp'), may hold values from 12.288 to 49.152
- up_square: float32 [960, 2560], P('group', 'dp'), may hold values from 30.72 to 122.88
- down_square: float32 [2560, 960], P('group', 'dp'), may hold values from 57.344 to 229.376
Outputs:
- output: float32 [4096, 960], P(('dp', 'group'))
- input_grad: float32 [4096, 960], P(('dp', 'group'))
- prenorm_grad: float32 [960], P('group')
- query_grad: float32 [960, 960], P('group', 'dp')
- key_grad: float32 [960, 320], P('group', 'dp')
- value_grad: float32 [960, 320], P('group', 'dp')
- out_grad: float32 [960, 960], P('group', 'dp')
- midnorm_grad: float32 [960], P('group')
- gate_grad: float32 [960, 2560], P('group', 'dp')
- up_grad: float32 [960, 2560], P('group', 'dp')
- down_grad: float32 [2560, 960], P('group', 'dp')
- prenorm_next: float32 [960], P('group')
- query_next: float32 [960, 960], P('group', 'dp')
- key_next: float32 [960, 320], P('group', 'dp')
- value_next: float32 [960, 320], P('group', 'dp')
- out_next: float32 [960, 960], P('group', 'dp')
- midnorm_next: float32 [960], P('group')
- gate_next: float32 [960, 2560], P('group', 'dp')
- up_next: float32 [960, 2560], P('group', 'dp')
- down_next: float32 [2560, 960], P('group', 'dp')
- prenorm_momentum: float32 [960], P('group')
- query_momentum: float32 [960, 960], P('group', 'dp')
- key_momentum: float32 [960, 320], P('group', 'dp')
- value_momentum: float32 [960, 320], P('group', 'dp')
- out_momentum: float32 [960, 960], P('group', 'dp')
- midnorm_momentum: float32 [960], P('group')
- gate_momentum: float32 [960, 2560], P('group', 'dp')
- up_momentum: float32 [960, 2560], P('group', 'dp')
- down_momentum: float32 [2560, 960], P('group', 'dp')
- prenorm_variance: float32 [960], P('group')
- query_variance: float32 [960, 960], P('group', 'dp')
- key_variance: float32 [960, 320], P('group', 'dp')
- value_variance: float32 [960, 320], P('group', 'dp')
- out_variance: float32 [960, 960], P('group', 'dp')
- midnorm_variance: float32 [960], P('group')
- gate_variance: float32 [960, 2560], P('group', 'dp')
- up_variance: float32 [960, 2560], P('group', 'dp')
- down_variance: float32 [2560, 960], P('group', 'dp')
The draws below stay inside these ranges and needn't reach their ends.
All inputs are finite; a program needn't handle non-finite values.
Results may differ from the reference program's by a relative error of at most 0.018.
Values may be sent and summed in bfloat16 or wider, within the bound.
No kernel may reach another device: no remote copies, remote signals or barrier semaphores. Data moves between devices by JAX's collectives and lax.ppermute only.
A program may use at most 128 MiB of HBM per device.

```python
import math
import jax
import jax.numpy as jnp
from jax import lax

MODEL_WIDTH = 960
QUERY_HEADS = 15
KEY_VALUE_HEADS = 5
HEAD_SIZE = 64
FF = 2560
SEQUENCE_LENGTH = 128
TOKENS = 4096


def shard_levels(stream_key, dims, shards, smallest, top_value):
    def one(axis_at, shards_of):
        draws = jax.random.uniform(jax.random.fold_in(jax.random.fold_in(stream_key, 6), axis_at), (shards_of,), jnp.float32, smallest / len(shards), top_value / len(shards))
        return jnp.repeat(jnp.exp(draws), dims[axis_at] // shards_of).reshape((-1,) + (1,) * (len(dims) - axis_at - 1))

    loudness = one(*shards[0])
    for cut in shards[1:]:
        loudness = loudness * one(*cut)
    return loudness


def normal_values(stream_key, dims, width, bound, cuts=(), kind=jnp.bfloat16):
    array = jax.random.normal(stream_key, dims, jnp.float32) * width
    if len(cuts) > 0:
        array = shard_levels(stream_key, dims, cuts, -0.22, 0.18) * array
    return jnp.clip(array, min=-bound, max=bound).astype(kind)


def setup_inputs(seed: int = 0) -> dict:
    seeds = jax.random.split(jax.random.key(seed), 30)
    return {
        "tokens": normal_values(seeds[0], (TOKENS, MODEL_WIDTH), 1.0, 6.0, ((0, 32),)),
        "cotangent": normal_values(seeds[1], (TOKENS, MODEL_WIDTH), 1.0, 6.0, ((0, 32),)),
        "prenorm_master": jnp.clip(1.0 + 0.1 * jax.random.normal(seeds[2], (MODEL_WIDTH,), jnp.float32), 0.5, 1.5),
        "query_master": normal_values(seeds[3], (MODEL_WIDTH, QUERY_HEADS * HEAD_SIZE), MODEL_WIDTH ** -0.5, 0.1875, ((0, 4), (1, 8)), jnp.float32),
        "key_master_copy": normal_values(seeds[4], (MODEL_WIDTH, KEY_VALUE_HEADS * HEAD_SIZE), MODEL_WIDTH ** -0.5, 0.1875, ((0, 4), (1, 8)), jnp.float32),
        "value_master_copy": normal_values(seeds[5], (MODEL_WIDTH, KEY_VALUE_HEADS * HEAD_SIZE), MODEL_WIDTH ** -0.5, 0.1875, ((0, 4), (1, 8)), jnp.float32),
        "out_master": normal_values(seeds[6], (QUERY_HEADS * HEAD_SIZE, MODEL_WIDTH), (QUERY_HEADS * HEAD_SIZE // 16) ** -0.5, 0.75, ((0, 4), (1, 8)), jnp.float32),
        "midnorm_master": jnp.clip(1.0 + 0.1 * jax.random.normal(seeds[7], (MODEL_WIDTH,), jnp.float32), 0.5, 1.5),
        "gate_master": normal_values(seeds[8], (MODEL_WIDTH, FF), MODEL_WIDTH ** -0.5, 0.1875, ((0, 4), (1, 8)), jnp.float32),
        "up_master": normal_values(seeds[9], (MODEL_WIDTH, FF), MODEL_WIDTH ** -0.5, 0.1875, ((0, 4), (1, 8)), jnp.float32),
        "down_master": normal_values(seeds[10], (FF, MODEL_WIDTH), FF ** -0.5, 0.125, ((0, 4), (1, 8)), jnp.float32),
        "prenorm_mean": normal_values(seeds[11], (MODEL_WIDTH,), (0.27 * TOKENS ** 0.5), 103.68, ((0, 4),), jnp.float32),
        "query_mean": normal_values(seeds[12], (MODEL_WIDTH, QUERY_HEADS * HEAD_SIZE), (0.21 * TOKENS ** 0.5), 80.64, ((0, 4), (1, 8)), jnp.float32),
        "key_first_moment": normal_values(seeds[13], (MODEL_WIDTH, KEY_VALUE_HEADS * HEAD_SIZE), (0.29 * TOKENS ** 0.5), 111.36, ((0, 4), (1, 8)), jnp.float32),
        "value_first_moment": normal_values(seeds[14], (MODEL_WIDTH, KEY_VALUE_HEADS * HEAD_SIZE), (0.31 * TOKENS ** 0.5), 119.04, ((0, 4), (1, 8)), jnp.float32),
        "out_mean": normal_values(seeds[15], (QUERY_HEADS * HEAD_SIZE, MODEL_WIDTH), (0.052 * TOKENS ** 0.5), 19.968, ((0, 4), (1, 8)), jnp.float32),
        "midnorm_mean": normal_values(seeds[16], (MODEL_WIDTH,), (0.12 * TOKENS ** 0.5), 46.08, ((0, 4),), jnp.float32),
        "gate_mean": normal_values(seeds[17], (MODEL_WIDTH, FF), (0.054 * TOKENS ** 0.5), 20.736, ((0, 4), (1, 8)), jnp.float32),
        "up_mean": normal_values(seeds[18], (MODEL_WIDTH, FF), (0.084 * TOKENS ** 0.5), 32.256, ((0, 4), (1, 8)), jnp.float32),
        "down_mean": normal_values(seeds[19], (FF, MODEL_WIDTH), (0.115 * TOKENS ** 0.5), 44.16, ((0, 4), (1, 8)), jnp.float32),
        "prenorm_square": jnp.clip(jnp.exp(math.log(1228.8) - 1.3862944 * jax.random.uniform(seeds[20], (MODEL_WIDTH,), jnp.float32) ** shard_levels(seeds[20], (MODEL_WIDTH,), ((0, 4),), -0.2, 0.2)), 307.2, 1228.8),
        "query_square": jnp.clip(jnp.exp(math.log(737.28) - 1.3862944 * jax.random.uniform(seeds[21], (MODEL_WIDTH, QUERY_HEADS * HEAD_SIZE), jnp.float32) ** shard_levels(seeds[21], (MODEL_WIDTH, QUERY_HEADS * HEAD_SIZE), ((0, 4), (1, 8)), -0.2, 0.2)), 184.32, 737.28),
        "key_second_moment": jnp.clip(jnp.exp(math.log(1474.56) - 1.3862944 * jax.random.uniform(seeds[22], (MODEL_WIDTH, KEY_VALUE_HEADS * HEAD_SIZE), jnp.float32) ** shard_levels(seeds[22], (MODEL_WIDTH, KEY_VALUE_HEADS * HEAD_SIZE), ((0, 4), (1, 8)), -0.2, 0.2)), 368.64, 1474.56),
        "value_second_moment": jnp.clip(jnp.exp(math.log(1638.4) - 1.3862944 * jax.random.uniform(seeds[23], (MODEL_WIDTH, KEY_VALUE_HEADS * HEAD_SIZE), jnp.float32) ** shard_levels(seeds[23], (MODEL_WIDTH, KEY_VALUE_HEADS * HEAD_SIZE), ((0, 4), (1, 8)), -0.2, 0.2)), 409.6, 1638.4),
        "out_square": jnp.clip(jnp.exp(math.log(49.152) - 1.3862944 * jax.random.uniform(seeds[24], (QUERY_HEADS * HEAD_SIZE, MODEL_WIDTH), jnp.float32) ** shard_levels(seeds[24], (QUERY_HEADS * HEAD_SIZE, MODEL_WIDTH), ((0, 4), (1, 8)), -0.2, 0.2)), 12.288, 49.152),
        "midnorm_square": jnp.clip(jnp.exp(math.log(245.76) - 1.3862944 * jax.random.uniform(seeds[25], (MODEL_WIDTH,), jnp.float32) ** shard_levels(seeds[25], (MODEL_WIDTH,), ((0, 4),), -0.2, 0.2)), 61.44, 245.76),
        "gate_square": jnp.clip(jnp.exp(math.log(49.152) - 1.3862944 * jax.random.uniform(seeds[26], (MODEL_WIDTH, FF), jnp.float32) ** shard_levels(seeds[26], (MODEL_WIDTH, FF), ((0, 4), (1, 8)), -0.2, 0.2)), 12.288, 49.152),
        "up_square": jnp.clip(jnp.exp(math.log(122.88) - 1.3862944 * jax.random.uniform(seeds[27], (MODEL_WIDTH, FF), jnp.float32) ** shard_levels(seeds[27], (MODEL_WIDTH, FF), ((0, 4), (1, 8)), -0.2, 0.2)), 30.72, 122.88),
        "down_square": jnp.clip(jnp.exp(math.log(229.376) - 1.3862944 * jax.random.uniform(seeds[28], (FF, MODEL_WIDTH), jnp.float32) ** shard_levels(seeds[28], (FF, MODEL_WIDTH), ((0, 4), (1, 8)), -0.2, 0.2)), 57.344, 229.376),
    }


EPS_NORM = 1e-05
BETA_ONE = 0.9
BETA_TWO = 0.95
ADAM_EPS = 1e-08
RATE_MATRIX = 0.015
RATE_OUTPUT = 0.05
RATE_GAIN = 0.4
DECAY_RATE = 0.1
ADAM_STEP = 4.0
ROPE_BASE = 10000.0

def weighted_values(pattern, left_op, right_op):
    return jnp.einsum(pattern, left_op.astype(jnp.float32), right_op.astype(jnp.float32))

def rotary_tables(length, head_dim):
    half_dim = head_dim // 2
    frequency = ROPE_BASE ** (-(jnp.arange(half_dim, dtype=jnp.float32) * 2.0 / head_dim))
    angles = jnp.arange(length, dtype=jnp.float32)[:, None] * frequency[None, :]
    return (jnp.cos(angles), jnp.sin(angles))

def apply_rotation(values, cosine_table, sine_table):
    half_dim = values.shape[-1] // 2
    first_half = values[..., :half_dim]
    second = values[..., half_dim:]
    cos_part = cosine_table[:, None, :]
    sin_part = sine_table[:, None, :]
    return jnp.concatenate([first_half * cos_part - second * sin_part, second * cos_part + first_half * sin_part], axis=-1)

def inverse_rotation(values, cosine_table, sine_table):
    half_dim = values.shape[-1] // 2
    first_half = values[..., :half_dim]
    second = values[..., half_dim:]
    cos_part = cosine_table[:, None, :]
    sin_part = sine_table[:, None, :]
    return jnp.concatenate([first_half * cos_part + second * sin_part, second * cos_part - first_half * sin_part], axis=-1)

def layer_pass(tokens, cotangent, gain_one, w_query, w_key, w_value, w_out, gain_two, w_gate, w_up, w_down):
    total_rows = tokens.shape[0]
    sequence_count = total_rows // SEQUENCE_LENGTH
    heads_per_group = QUERY_HEADS // KEY_VALUE_HEADS
    score_scale = HEAD_SIZE ** (-0.5)
    tok_float = tokens.astype(jnp.float32)
    inv_one = lax.rsqrt(lax.optimization_barrier(jnp.mean(tok_float * tok_float, axis=-1, keepdims=True)) + EPS_NORM)
    scaled_one = tok_float * inv_one
    gain_first = gain_one.astype(jnp.float32)
    normed_one = (scaled_one * gain_first).astype(jnp.bfloat16)
    query_raw = jnp.dot(normed_one, w_query, preferred_element_type=jnp.float32)
    key_unrotated = jnp.dot(normed_one, w_key, preferred_element_type=jnp.float32)
    value_projected = jnp.dot(normed_one, w_value, preferred_element_type=jnp.float32)
    cosine_table, sine_table = rotary_tables(SEQUENCE_LENGTH, HEAD_SIZE)
    query_rotated = apply_rotation(query_raw.reshape(sequence_count, SEQUENCE_LENGTH, QUERY_HEADS, HEAD_SIZE), cosine_table, sine_table).astype(jnp.bfloat16)
    query_grouped = query_rotated.reshape(sequence_count, SEQUENCE_LENGTH, KEY_VALUE_HEADS, heads_per_group, HEAD_SIZE)
    key_rotated = apply_rotation(key_unrotated.reshape(sequence_count, SEQUENCE_LENGTH, KEY_VALUE_HEADS, HEAD_SIZE), cosine_table, sine_table).astype(jnp.bfloat16)
    value_reduced = value_projected.reshape(sequence_count, SEQUENCE_LENGTH, KEY_VALUE_HEADS, HEAD_SIZE).astype(jnp.bfloat16)
    scores = weighted_values('sqkgd,spkd->skgqp', query_grouped, key_rotated) * score_scale
    causal = jnp.arange(SEQUENCE_LENGTH)[:, None] >= jnp.arange(SEQUENCE_LENGTH)[None, :]
    raw_weights = jnp.where(causal, jnp.exp(scores), 0.0)
    prob_full = raw_weights / lax.optimization_barrier(jnp.sum(raw_weights, axis=-1, keepdims=True))
    probability_reduced = prob_full.astype(jnp.bfloat16)
    attended = weighted_values('skgqp,spkd->sqkgd', probability_reduced, value_reduced)
    attended_low = attended.reshape(total_rows, QUERY_HEADS * HEAD_SIZE).astype(jnp.bfloat16)
    middle = tok_float + jnp.dot(attended_low, w_out, preferred_element_type=jnp.float32)
    inv_two = lax.rsqrt(lax.optimization_barrier(jnp.mean(middle * middle, axis=-1, keepdims=True)) + EPS_NORM)
    scaled_two = middle * inv_two
    gain_second = gain_two.astype(jnp.float32)
    normed_two = (scaled_two * gain_second).astype(jnp.bfloat16)
    gate_value = jnp.dot(normed_two, w_gate, preferred_element_type=jnp.float32)
    up_value = jnp.dot(normed_two, w_up, preferred_element_type=jnp.float32)
    sigmoid_gate = jax.nn.sigmoid(gate_value)
    silu_gate = gate_value * sigmoid_gate
    hidden = (silu_gate * up_value).astype(jnp.bfloat16)
    output = middle + jnp.dot(hidden, w_down, preferred_element_type=jnp.float32)
    cot_float = cotangent.astype(jnp.float32)
    down_sum = jnp.dot(hidden.T, cotangent, preferred_element_type=jnp.float32)
    d_hidden = jnp.dot(cotangent, w_down.T, preferred_element_type=jnp.float32)
    d_gate = (d_hidden * up_value * sigmoid_gate * (1.0 + gate_value * (1.0 - sigmoid_gate))).astype(jnp.bfloat16)
    d_up = (d_hidden * silu_gate).astype(jnp.bfloat16)
    gate_sum = jnp.dot(normed_two.T, d_gate, preferred_element_type=jnp.float32)
    up_sum = jnp.dot(normed_two.T, d_up, preferred_element_type=jnp.float32)
    d_normed_two = jnp.dot(d_gate, w_gate.T, preferred_element_type=jnp.float32) + jnp.dot(d_up, w_up.T, preferred_element_type=jnp.float32)
    midnorm_sum = lax.optimization_barrier(jnp.sum(d_normed_two * scaled_two, axis=0))
    d_scaled_two = d_normed_two * gain_second
    d_middle = cot_float + inv_two * (d_scaled_two - scaled_two * lax.optimization_barrier(jnp.mean(d_scaled_two * scaled_two, axis=-1, keepdims=True)))
    d_middle_low = d_middle.astype(jnp.bfloat16)
    out_sum = jnp.dot(attended_low.T, d_middle_low, preferred_element_type=jnp.float32)
    attended_gradient = jnp.dot(d_middle_low, w_out.T, preferred_element_type=jnp.float32).astype(jnp.bfloat16)
    attended_gradient = attended_gradient.reshape(sequence_count, SEQUENCE_LENGTH, KEY_VALUE_HEADS, heads_per_group, HEAD_SIZE)
    d_prob = weighted_values('sqkgd,spkd->skgqp', attended_gradient, value_reduced)
    inner_sum = lax.optimization_barrier(jnp.sum(prob_full * d_prob, axis=-1, keepdims=True))
    d_score = (prob_full * (d_prob - inner_sum) * score_scale).astype(jnp.bfloat16)
    d_query = weighted_values('skgqp,spkd->sqkgd', d_score, key_rotated).reshape(sequence_count, SEQUENCE_LENGTH, QUERY_HEADS, HEAD_SIZE)
    d_query = inverse_rotation(d_query, cosine_table, sine_table).reshape(total_rows, QUERY_HEADS * HEAD_SIZE).astype(jnp.bfloat16)
    key_gradient = weighted_values('fceti,ftcel->ficl', d_score, query_grouped)
    key_gradient = inverse_rotation(key_gradient, cosine_table, sine_table).reshape(total_rows, KEY_VALUE_HEADS * HEAD_SIZE).astype(jnp.bfloat16)
    value_gradient = weighted_values('fceti,ftcel->ficl', probability_reduced, attended_gradient).reshape(total_rows, KEY_VALUE_HEADS * HEAD_SIZE).astype(jnp.bfloat16)
    query_sum = jnp.dot(normed_one.T, d_query, preferred_element_type=jnp.float32)
    key_sum = jnp.dot(normed_one.T, key_gradient, preferred_element_type=jnp.float32)
    value_sum = jnp.dot(normed_one.T, value_gradient, preferred_element_type=jnp.float32)
    d_normed_one = jnp.dot(d_query, w_query.T, preferred_element_type=jnp.float32) + jnp.dot(key_gradient, w_key.T, preferred_element_type=jnp.float32) + jnp.dot(value_gradient, w_value.T, preferred_element_type=jnp.float32)
    prenorm_sum = lax.optimization_barrier(jnp.sum(d_normed_one * scaled_one, axis=0))
    d_scaled_one = d_normed_one * gain_first
    input_grad = d_middle + inv_one * (d_scaled_one - scaled_one * lax.optimization_barrier(jnp.mean(d_scaled_one * scaled_one, axis=-1, keepdims=True)))
    return (output, input_grad, (prenorm_sum, query_sum, key_sum, value_sum, out_sum, midnorm_sum, gate_sum, up_sum, down_sum))

def adam_update(master, mean_old, square_old, gradient, rate, decay):
    momentum = BETA_ONE * mean_old + (1.0 - BETA_ONE) * gradient
    variance = BETA_TWO * square_old + (1.0 - BETA_TWO) * gradient * gradient
    fix_one = 1.0 - BETA_ONE ** ADAM_STEP
    fix_two = 1.0 - BETA_TWO ** ADAM_STEP
    update = momentum / fix_one / (jnp.sqrt(variance / fix_two) + ADAM_EPS) + decay * master
    return (master - rate * update, momentum, variance)

def reference(tokens, cotangent, prenorm_master, query_master, key_master_copy, value_master_copy, out_master, midnorm_master, gate_master, up_master, down_master, prenorm_mean, query_mean, key_first_moment, value_first_moment, out_mean, midnorm_mean, gate_mean, up_mean, down_mean, prenorm_square, query_square, key_second_moment, value_second_moment, out_square, midnorm_square, gate_square, up_square, down_square):
    masters = (prenorm_master, query_master, key_master_copy, value_master_copy, out_master, midnorm_master, gate_master, up_master, down_master)
    low_weights = tuple((piece.astype(jnp.bfloat16) for piece in masters))
    block_rows = math.gcd(TOKENS, 4096)
    blocks = TOKENS // block_rows

    def add_block(running, pieces):
        tok_block, cot_block = pieces
        out_block, grad_block, block_sums = layer_pass(tok_block, cot_block, *low_weights)
        return (tuple((old_total + new_term for old_total, new_term in zip(running, block_sums))), (out_block, grad_block))
    initial = tuple((jnp.zeros(piece.shape, jnp.float32) for piece in masters))
    totals, (outputs, grads) = lax.scan(add_block, initial, (tokens.reshape(blocks, block_rows, MODEL_WIDTH), cotangent.reshape(blocks, block_rows, MODEL_WIDTH)))
    mean_list = (prenorm_mean, query_mean, key_first_moment, value_first_moment, out_mean, midnorm_mean, gate_mean, up_mean, down_mean)
    square_list = (prenorm_square, query_square, key_second_moment, value_second_moment, out_square, midnorm_square, gate_square, up_square, down_square)
    rate_list = (RATE_GAIN, RATE_MATRIX, RATE_MATRIX, RATE_MATRIX, RATE_OUTPUT, RATE_GAIN, RATE_MATRIX, RATE_MATRIX, RATE_MATRIX)
    decays = (0.0, DECAY_RATE, DECAY_RATE, DECAY_RATE, DECAY_RATE, 0.0, DECAY_RATE, DECAY_RATE, DECAY_RATE)
    results = [adam_update(masters[k], mean_list[k], square_list[k], totals[k], rate_list[k], decays[k]) for k in range(9)]
    return (outputs.reshape(TOKENS, MODEL_WIDTH), grads.reshape(TOKENS, MODEL_WIDTH), totals[0], totals[1], totals[2], totals[3], totals[4], totals[5], totals[6], totals[7], totals[8], results[0][0], results[1][0], results[2][0], results[3][0], results[4][0], results[5][0], results[6][0], results[7][0], results[8][0], results[0][1], results[1][1], results[2][1], results[3][1], results[4][1], results[5][1], results[6][1], results[7][1], results[8][1], results[0][2], results[1][2], results[2][2], results[3][2], results[4][2], results[5][2], results[6][2], results[7][2], results[8][2])
```

```python
import jax
import jax.numpy as jnp
from jax import lax
from jax.sharding import PartitionSpec as P

QUERY_HEADS = 15
KEY_VALUE_HEADS = 5
HEAD_SIZE = 64
SEQUENCE_LENGTH = 128


EPS_NORM = 1e-05
BETA_ONE = 0.9
BETA_TWO = 0.95
ADAM_EPS = 1e-08
RATE_MATRIX = 0.015
RATE_OUTPUT = 0.05
RATE_GAIN = 0.4
DECAY_RATE = 0.1
ADAM_STEP = 4.0
ROPE_BASE = 10000.0


def weighted_values(pattern, left_op, right_op):
    return jnp.einsum(pattern, left_op, right_op, preferred_element_type=jnp.float32)


def rotary_tables(length, head_dim):
    half_dim = head_dim // 2
    frequency = ROPE_BASE ** (-(jnp.arange(half_dim, dtype=jnp.float32) * 2.0 / head_dim))
    angles = jnp.arange(length, dtype=jnp.float32)[:, None] * frequency[None, :]
    return (jnp.cos(angles), jnp.sin(angles))


def apply_rotation(values, cosine_table, sine_table):
    half_dim = values.shape[-1] // 2
    first_half = values[..., :half_dim]
    second = values[..., half_dim:]
    cos_part = cosine_table[:, None, :]
    sin_part = sine_table[:, None, :]
    return jnp.concatenate(
        [first_half * cos_part - second * sin_part, second * cos_part + first_half * sin_part],
        axis=-1,
    )


def inverse_rotation(values, cosine_table, sine_table):
    half_dim = values.shape[-1] // 2
    first_half = values[..., :half_dim]
    second = values[..., half_dim:]
    cos_part = cosine_table[:, None, :]
    sin_part = sine_table[:, None, :]
    return jnp.concatenate(
        [first_half * cos_part + second * sin_part, second * cos_part - first_half * sin_part],
        axis=-1,
    )


def swap(value, axis, bit, size):
    return lax.ppermute(value, axis, [(i, i ^ bit) for i in range(size)])


def gather_relative(value, axis, size, bits):
    held, order = value[None], [0]
    for bit in bits:
        held = jnp.concatenate([held, swap(held, axis, bit, size)], axis=0)
        order = order + [r ^ bit for r in order]
    return held, order


def reduce_relative(held, axis, size, bits, order):
    for bit in bits:
        count = held.shape[0] // 2
        got = swap(held[count:].astype(jnp.bfloat16), axis, bit, size)
        held = held[:count].astype(jnp.float32) + got.astype(jnp.float32)
    return held[0]


def pick(blocks, order, place):
    rank = [order.index(j) for j in range(len(order))]
    table = jnp.asarray(rank, jnp.int32)
    wanted = table[jnp.arange(len(order), dtype=jnp.int32) ^ place]
    return jnp.take(blocks, wanted, axis=0, mode="clip")


def unpick(blocks, order, place):
    wanted = jnp.asarray(order, jnp.int32) ^ place
    return jnp.take(blocks, wanted, axis=0, mode="clip")


def dot(left_op, right_op, left_dim, right_dim):
    return lax.dot_general(
        left_op, right_op, (((left_dim,), (right_dim,)), ((), ())), preferred_element_type=jnp.float32
    )


def split_features(values, parts):
    width = values.shape[1] // parts
    return jnp.stack([values[:, i * width : (i + 1) * width] for i in range(parts)])


def join_features(blocks):
    return jnp.concatenate([blocks[i] for i in range(blocks.shape[0])], axis=1)


def adam_update(master, mean_old, square_old, gradient, rate, decay):
    momentum = BETA_ONE * mean_old + (1.0 - BETA_ONE) * gradient
    variance = BETA_TWO * square_old + (1.0 - BETA_TWO) * gradient * gradient
    fix_one = 1.0 - BETA_ONE**ADAM_STEP
    fix_two = 1.0 - BETA_TWO**ADAM_STEP
    update = momentum / fix_one / (jnp.sqrt(variance / fix_two) + ADAM_EPS) + decay * master
    return (master - rate * update, momentum, variance)


def per_device(
    tokens,
    cotangent,
    prenorm_master,
    query_master,
    key_master_copy,
    value_master_copy,
    out_master,
    midnorm_master,
    gate_master,
    up_master,
    down_master,
    prenorm_mean,
    query_mean,
    key_first_moment,
    value_first_moment,
    out_mean,
    midnorm_mean,
    gate_mean,
    up_mean,
    down_mean,
    prenorm_square,
    query_square,
    key_second_moment,
    value_second_moment,
    out_square,
    midnorm_square,
    gate_square,
    up_square,
    down_square,
):
    masters = (
        prenorm_master,
        query_master,
        key_master_copy,
        value_master_copy,
        out_master,
        midnorm_master,
        gate_master,
        up_master,
        down_master,
    )
    low = jnp.bfloat16
    n_group, n_dp = lax.axis_size("group"), lax.axis_size("dp")
    my_group, my_dp = lax.axis_index("group"), lax.axis_index("dp")
    group_bits = [1 << i for i in range(n_group.bit_length() - 1)][::-1]
    dp_bits = [1 << i for i in range(n_dp.bit_length() - 1)][::-1]

    def gather_dp(block):
        held, order = gather_relative(block, "dp", n_dp, dp_bits)
        return pick(held, order, my_dp)

    def gather_group(block):
        return gather_relative(block, "group", n_group, group_bits)

    xors = [0]
    for bit in dp_bits:
        xors = xors + [r ^ bit for r in xors]
    dp_order = xors
    xors = [0]
    for bit in group_bits:
        xors = xors + [r ^ bit for r in xors]
    group_order = xors

    def reduce_dp(blocks):
        return reduce_relative(unpick(blocks, dp_order, my_dp), "dp", n_dp, dp_bits[::-1], dp_order)

    def reduce_group(blocks):
        return reduce_relative(blocks, "group", n_group, group_bits[::-1], group_order)

    rows = tokens.shape[0]
    width = tokens.shape[1]
    part = width // n_group
    gains = jnp.stack([prenorm_master, midnorm_master]).astype(low)
    gains_held, _ = gather_group(gains)
    gains_all = join_features(pick(gains_held, group_order, my_group)).astype(jnp.float32)
    gain_first, gain_second = gains_all[0:1], gains_all[1:2]

    def gather_full(parts_list):
        block = jnp.concatenate([p.astype(low).T for p in parts_list], axis=0)
        sizes = [p.shape[1] for p in parts_list]
        columns = gather_dp(block)
        start, pieces = 0, []
        for size in sizes:
            pieces.append(columns[:, start : start + size, :].reshape(n_dp * size, part))
            start += size
        joined = pieces[0] if len(pieces) == 1 else jnp.concatenate(pieces, axis=0)
        return gather_group(joined)[0]

    w_query_t = gather_full([query_master])
    w_kv_t = gather_full([key_master_copy, value_master_copy])
    w_out_t = gather_full([out_master])

    unit = gate_master.shape[1] // (n_group)
    unit_rows = n_dp // n_group

    def to_units(weight):
        block = weight.astype(low).T.reshape(n_group, unit, part)
        block = lax.all_to_all(block, "group", 0, 0, tiled=True)
        return join_features(block)

    gate_block, up_block = to_units(gate_master), to_units(up_master)
    down_cols = down_master.shape[1]
    down_block = down_master.astype(low).reshape(unit_rows, n_group, unit, down_cols)
    down_block = down_block.transpose(1, 0, 2, 3).reshape(n_group, unit_rows * unit, down_cols)
    down_block = lax.all_to_all(down_block, "group", 0, 0, tiled=True)
    down_block = down_block.reshape(n_dp * unit, down_cols).T
    w_gate_t = gather_dp(gate_block).reshape(n_dp * unit, width)
    w_up_t = gather_dp(up_block).reshape(n_dp * unit, width)
    w_down_t = gather_dp(down_block).reshape(width, n_dp * unit)

    cot_held = gather_group(cotangent)[0].reshape(n_group * rows, width)

    sequence_count = rows // SEQUENCE_LENGTH
    heads_per_group = QUERY_HEADS // KEY_VALUE_HEADS
    score_scale = HEAD_SIZE ** (-0.5)
    q_width = QUERY_HEADS * HEAD_SIZE
    k_width = KEY_VALUE_HEADS * HEAD_SIZE
    tok_float = tokens.astype(jnp.float32)
    inv_one = lax.rsqrt(jnp.mean(tok_float * tok_float, axis=-1, keepdims=True) + EPS_NORM)
    scaled_one = tok_float * inv_one
    normed_one = (scaled_one * gain_first).astype(low)
    normed_rel = unpick(split_features(normed_one, n_group), group_order, my_group)

    def project(blocks, weights):
        total = dot(blocks[0], weights[0], 1, 1)
        for r in range(1, n_group):
            total = total + dot(blocks[r], weights[r], 1, 1)
        return total

    query_raw = project(normed_rel, w_query_t)
    kv_raw = project(normed_rel, w_kv_t)
    key_unrotated, value_projected = kv_raw[:, :k_width], kv_raw[:, k_width:]
    cosine_table, sine_table = rotary_tables(SEQUENCE_LENGTH, HEAD_SIZE)
    query_rotated = apply_rotation(
        query_raw.reshape(sequence_count, SEQUENCE_LENGTH, QUERY_HEADS, HEAD_SIZE),
        cosine_table,
        sine_table,
    ).astype(low)
    query_grouped = query_rotated.reshape(
        sequence_count, SEQUENCE_LENGTH, KEY_VALUE_HEADS, heads_per_group, HEAD_SIZE
    )
    key_rotated = apply_rotation(
        key_unrotated.reshape(sequence_count, SEQUENCE_LENGTH, KEY_VALUE_HEADS, HEAD_SIZE),
        cosine_table,
        sine_table,
    ).astype(low)
    value_reduced = value_projected.reshape(
        sequence_count, SEQUENCE_LENGTH, KEY_VALUE_HEADS, HEAD_SIZE
    ).astype(low)
    scores = weighted_values("sqkgd,spkd->skgqp", query_grouped, key_rotated) * score_scale
    causal = jnp.arange(SEQUENCE_LENGTH)[:, None] >= jnp.arange(SEQUENCE_LENGTH)[None, :]
    raw_weights = jnp.where(causal, jnp.exp(scores), 0.0)
    prob_full = raw_weights / jnp.sum(raw_weights, axis=-1, keepdims=True)
    probability_reduced = prob_full.astype(low)
    attended = weighted_values("skgqp,spkd->sqkgd", probability_reduced, value_reduced)
    attended_low = attended.reshape(rows, q_width).astype(low)
    attended_rel = unpick(split_features(attended_low, n_group), group_order, my_group)
    middle = tok_float + project(attended_rel, w_out_t)
    inv_two = lax.rsqrt(jnp.mean(middle * middle, axis=-1, keepdims=True) + EPS_NORM)
    scaled_two = middle * inv_two
    normed_two = (scaled_two * gain_second).astype(low)
    normed_all = gather_group(normed_two)[0].reshape(n_group * rows, width)
    d_hidden = dot(cot_held, w_down_t, 1, 0)
    gate_value = dot(normed_all, w_gate_t, 1, 1)
    up_value = dot(normed_all, w_up_t, 1, 1)
    sigmoid_gate = jax.nn.sigmoid(gate_value)
    silu_gate = gate_value * sigmoid_gate
    hidden = (silu_gate * up_value).astype(low)
    d_gate = (
        d_hidden * up_value * sigmoid_gate * (1.0 + gate_value * (1.0 - sigmoid_gate))
    ).astype(low)
    d_up = (d_hidden * silu_gate).astype(low)
    d_normed_part = dot(d_gate, w_gate_t, 1, 0) + dot(d_up, w_up_t, 1, 0)
    d_normed_two = reduce_group(d_normed_part.astype(low).reshape(n_group, rows, width))

    gate_sum = reduce_dp(dot(d_gate, normed_all, 0, 0).astype(low).reshape(n_dp, unit, width))
    up_sum = reduce_dp(dot(d_up, normed_all, 0, 0).astype(low).reshape(n_dp, unit, width))
    down_sum = reduce_dp(dot(cot_held, hidden, 0, 0).astype(low).reshape(n_dp, down_cols, n_dp * unit))
    out_part = dot(hidden, w_down_t, 1, 1)
    output = middle + reduce_group(out_part.astype(low).reshape(n_group, rows, width))

    def from_units(total):
        block = split_features(total.astype(low), n_group)
        block = lax.all_to_all(block, "group", 0, 0, tiled=True)
        return block.reshape(n_group * unit, part).T.astype(jnp.float32)

    gate_own, up_own = from_units(gate_sum), from_units(up_sum)
    down_back = down_sum.astype(low).T.reshape(n_group, unit_rows * unit, down_cols)
    down_back = lax.all_to_all(down_back, "group", 0, 0, tiled=True)
    down_back = down_back.reshape(n_group, unit_rows, unit, down_cols).transpose(1, 0, 2, 3)
    down_own = down_back.reshape(n_dp * unit, down_cols).astype(jnp.float32)

    cot_float = cotangent.astype(jnp.float32)
    midnorm_sum = jnp.sum(d_normed_two * scaled_two, axis=0, keepdims=True)
    d_scaled_two = d_normed_two * gain_second
    d_middle = cot_float + inv_two * (
        d_scaled_two - scaled_two * jnp.mean(d_scaled_two * scaled_two, axis=-1, keepdims=True)
    )
    d_middle_low = d_middle.astype(low)

    def weight_grad(columns, blocks):
        return jnp.stack([dot(columns, blocks[r], 0, 0).astype(low) for r in range(n_group)])

    def input_part(columns, weights):
        return jnp.stack([dot(columns, weights[r], 1, 0) for r in range(n_group)])

    out_sum = reduce_group(weight_grad(d_middle_low, attended_rel))
    out_own = reduce_dp(out_sum.astype(low).reshape(n_dp, width // n_dp, part)).T
    attended_gradient = join_features(
        pick(input_part(d_middle_low, w_out_t).astype(low), group_order, my_group)
    )
    attended_gradient = attended_gradient.reshape(
        sequence_count, SEQUENCE_LENGTH, KEY_VALUE_HEADS, heads_per_group, HEAD_SIZE
    )
    d_prob = weighted_values("sqkgd,spkd->skgqp", attended_gradient, value_reduced)
    inner_sum = jnp.sum(prob_full * d_prob, axis=-1, keepdims=True)
    d_score = (prob_full * (d_prob - inner_sum) * score_scale).astype(low)
    d_query = weighted_values("skgqp,spkd->sqkgd", d_score, key_rotated).reshape(
        sequence_count, SEQUENCE_LENGTH, QUERY_HEADS, HEAD_SIZE
    )
    d_query = inverse_rotation(d_query, cosine_table, sine_table).reshape(rows, q_width).astype(low)
    key_gradient = weighted_values("fceti,ftcel->ficl", d_score, query_grouped)
    key_gradient = (
        inverse_rotation(key_gradient, cosine_table, sine_table).reshape(rows, k_width).astype(low)
    )
    value_gradient = (
        weighted_values("fceti,ftcel->ficl", probability_reduced, attended_gradient)
        .reshape(rows, k_width)
        .astype(low)
    )
    kv_gradient = jnp.concatenate([key_gradient, value_gradient], axis=1)
    query_sum = reduce_group(weight_grad(d_query, normed_rel))
    query_own = reduce_dp(query_sum.astype(low).reshape(n_dp, q_width // n_dp, part)).T
    kv_sum = weight_grad(kv_gradient, normed_rel)
    d_normed_blocks = input_part(d_query, w_query_t) + input_part(kv_gradient, w_kv_t)
    d_normed_one = join_features(pick(d_normed_blocks, group_order, my_group))
    prenorm_sum = jnp.sum(d_normed_one * scaled_one, axis=0, keepdims=True)
    d_scaled_one = d_normed_one * gain_first
    input_grad = d_middle + inv_one * (
        d_scaled_one - scaled_one * jnp.mean(d_scaled_one * scaled_one, axis=-1, keepdims=True)
    )

    gain_rows = jnp.concatenate([prenorm_sum, midnorm_sum], axis=0)
    gain_rel = unpick(split_features(gain_rows, n_group), group_order, my_group)
    gain_own = reduce_group(gain_rel)
    for bit in dp_bits:
        mine = gain_own.astype(low)
        gain_own = mine.astype(jnp.float32) + swap(mine, "dp", bit, n_dp).astype(jnp.float32)
    prenorm_own, midnorm_own = gain_own[0], gain_own[1]

    kv_group = reduce_group(kv_sum)
    k_cols = k_width // n_dp
    kv_blocks = jnp.concatenate(
        [
            kv_group[:k_width].reshape(n_dp, k_cols, part),
            kv_group[k_width:].reshape(n_dp, k_cols, part),
        ],
        axis=1,
    ).astype(low)
    kv_own = reduce_dp(kv_blocks)
    key_own, value_own = kv_own[:k_cols].T, kv_own[k_cols:].T
    owned = (
        prenorm_own,
        query_own,
        key_own,
        value_own,
        out_own,
        midnorm_own,
        gate_own,
        up_own,
        down_own,
    )
    mean_list = (
        prenorm_mean,
        query_mean,
        key_first_moment,
        value_first_moment,
        out_mean,
        midnorm_mean,
        gate_mean,
        up_mean,
        down_mean,
    )
    square_list = (
        prenorm_square,
        query_square,
        key_second_moment,
        value_second_moment,
        out_square,
        midnorm_square,
        gate_square,
        up_square,
        down_square,
    )
    rate_list = (
        RATE_GAIN,
        RATE_MATRIX,
        RATE_MATRIX,
        RATE_MATRIX,
        RATE_OUTPUT,
        RATE_GAIN,
        RATE_MATRIX,
        RATE_MATRIX,
        RATE_MATRIX,
    )
    decays = (
        0.0,
        DECAY_RATE,
        DECAY_RATE,
        DECAY_RATE,
        DECAY_RATE,
        0.0,
        DECAY_RATE,
        DECAY_RATE,
        DECAY_RATE,
    )
    results = [
        adam_update(masters[k], mean_list[k], square_list[k], owned[k], rate_list[k], decays[k])
        for k in range(9)
    ]
    return (
        output,
        input_grad,
        owned[0],
        owned[1],
        owned[2],
        owned[3],
        owned[4],
        owned[5],
        owned[6],
        owned[7],
        owned[8],
        results[0][0],
        results[1][0],
        results[2][0],
        results[3][0],
        results[4][0],
        results[5][0],
        results[6][0],
        results[7][0],
        results[8][0],
        results[0][1],
        results[1][1],
        results[2][1],
        results[3][1],
        results[4][1],
        results[5][1],
        results[6][1],
        results[7][1],
        results[8][1],
        results[0][2],
        results[1][2],
        results[2][2],
        results[3][2],
        results[4][2],
        results[5][2],
        results[6][2],
        results[7][2],
        results[8][2],
    )


def solution(mesh):
    placed = (
        P(("dp", "group"), None),
        P(("dp", "group"), None),
        P("group"),
        P("group", "dp"),
        P("group", "dp"),
        P("group", "dp"),
        P("group", "dp"),
        P("group"),
        P("group", "dp"),
        P("group", "dp"),
        P("group", "dp"),
        P("group"),
        P("group", "dp"),
        P("group", "dp"),
        P("group", "dp"),
        P("group", "dp"),
        P("group"),
        P("group", "dp"),
        P("group", "dp"),
        P("group", "dp"),
        P("group"),
        P("group", "dp"),
        P("group", "dp"),
        P("group", "dp"),
        P("group", "dp"),
        P("group"),
        P("group", "dp"),
        P("group", "dp"),
        P("group", "dp"),
    )
    return jax.shard_map(
        per_device,
        mesh=mesh,
        in_specs=placed,
        out_specs=(
            P(("dp", "group"), None),
            P(("dp", "group"), None),
            P("group"),
            P("group", "dp"),
            P("group", "dp"),
            P("group", "dp"),
            P("group", "dp"),
            P("group"),
            P("group", "dp"),
            P("group", "dp"),
            P("group", "dp"),
            P("group"),
            P("group", "dp"),
            P("group", "dp"),
            P("group", "dp"),
            P("group", "dp"),
            P("group"),
            P("group", "dp"),
            P("group", "dp"),
            P("group", "dp"),
            P("group"),
            P("group", "dp"),
            P("group", "dp"),
            P("group", "dp"),
            P("group", "dp"),
            P("group"),
            P("group", "dp"),
            P("group", "dp"),
            P("group", "dp"),
            P("group"),
            P("group", "dp"),
            P("group", "dp"),
            P("group", "dp"),
            P("group", "dp"),
            P("group"),
            P("group", "dp"),
            P("group", "dp"),
            P("group", "dp"),
        ),
        check_vma=False,
    )
```

```python
import jax
import jax.numpy as jnp
from jax import lax
from jax.sharding import PartitionSpec as P

QUERY_HEADS = 15
KEY_VALUE_HEADS = 5
HEAD_SIZE = 64
SEQUENCE_LENGTH = 128


EPS_NORM = 1e-05
BETA_ONE = 0.9
BETA_TWO = 0.95
ADAM_EPS = 1e-08
RATE_MATRIX = 0.015
RATE_OUTPUT = 0.05
RATE_GAIN = 0.4
DECAY_RATE = 0.1
ADAM_STEP = 4.0
ROPE_BASE = 10000.0


def weighted_values(pattern, left_op, right_op):
    return jnp.einsum(pattern, left_op, right_op, preferred_element_type=jnp.float32)


def rotary_tables(length, head_dim):
    half_dim = head_dim // 2
    frequency = ROPE_BASE ** (-(jnp.arange(half_dim, dtype=jnp.float32) * 2.0 / head_dim))
    angles = jnp.arange(length, dtype=jnp.float32)[:, None] * frequency[None, :]
    return (jnp.cos(angles), jnp.sin(angles))


def apply_rotation(values, cosine_table, sine_table):
    half_dim = values.shape[-1] // 2
    first_half = values[..., :half_dim]
    second = values[..., half_dim:]
    cos_part = cosine_table[:, None, :]
    sin_part = sine_table[:, None, :]
    return jnp.concatenate(
        [first_half * cos_part - second * sin_part, second * cos_part + first_half * sin_part],
        axis=-1,
    )


def inverse_rotation(values, cosine_table, sine_table):
    half_dim = values.shape[-1] // 2
    first_half = values[..., :half_dim]
    second = values[..., half_dim:]
    cos_part = cosine_table[:, None, :]
    sin_part = sine_table[:, None, :]
    return jnp.concatenate(
        [first_half * cos_part + second * sin_part, second * cos_part - first_half * sin_part],
        axis=-1,
    )


def swap(value, axis, bit, size):
    return lax.ppermute(value, axis, [(i, i ^ bit) for i in range(size)])


def gather_steps(value, steps, sizes, places):
    held, done = value, []
    for axis, bit in steps:
        got = swap(held, axis, bit, sizes[axis])
        upper = (places[axis] & bit) != 0
        at = len([d for d in done if (d[0] == "dp" and axis == "group") or (d[0] == axis and d[1] > bit)])
        low_part, high_part = jnp.where(upper, got, held), jnp.where(upper, held, got)
        held = jnp.stack([low_part, high_part], axis=at)
        done = done + [(axis, bit)]
    return held


def reduce_steps(value, steps, sizes, places, done):
    held, done = value, list(done)
    for axis, bit in steps:
        at = done.index((axis, bit))
        mine = ((places[axis] & bit) != 0).astype(jnp.int32)
        sent = lax.dynamic_index_in_dim(held, 1 - mine, at, keepdims=False).astype(jnp.bfloat16)
        kept = lax.dynamic_index_in_dim(held, mine, at, keepdims=False)
        got = swap(sent, axis, bit, sizes[axis])
        held = (kept.astype(jnp.float32) + got.astype(jnp.float32)).astype(jnp.bfloat16)
        done.pop(at)
        last = kept.astype(jnp.float32) + got.astype(jnp.float32)
    return last


def dot(left_op, right_op, left_dim, right_dim):
    return lax.dot_general(
        left_op, right_op, (((left_dim,), (right_dim,)), ((), ())), preferred_element_type=jnp.float32
    )


def split_features(values, parts):
    width = values.shape[1] // parts
    return jnp.stack([values[:, i * width : (i + 1) * width] for i in range(parts)])


def join_features(blocks):
    return jnp.concatenate([blocks[i] for i in range(blocks.shape[0])], axis=1)


def adam_update(master, mean_old, square_old, gradient, rate, decay):
    momentum = BETA_ONE * mean_old + (1.0 - BETA_ONE) * gradient
    variance = BETA_TWO * square_old + (1.0 - BETA_TWO) * gradient * gradient
    fix_one = 1.0 - BETA_ONE**ADAM_STEP
    fix_two = 1.0 - BETA_TWO**ADAM_STEP
    update = momentum / fix_one / (jnp.sqrt(variance / fix_two) + ADAM_EPS) + decay * master
    return (master - rate * update, momentum, variance)


def per_device(
    tokens,
    cotangent,
    prenorm_master,
    query_master,
    key_master_copy,
    value_master_copy,
    out_master,
    midnorm_master,
    gate_master,
    up_master,
    down_master,
    prenorm_mean,
    query_mean,
    key_first_moment,
    value_first_moment,
    out_mean,
    midnorm_mean,
    gate_mean,
    up_mean,
    down_mean,
    prenorm_square,
    query_square,
    key_second_moment,
    value_second_moment,
    out_square,
    midnorm_square,
    gate_square,
    up_square,
    down_square,
):
    masters = (
        prenorm_master,
        query_master,
        key_master_copy,
        value_master_copy,
        out_master,
        midnorm_master,
        gate_master,
        up_master,
        down_master,
    )
    low = jnp.bfloat16
    n_group, n_dp = lax.axis_size("group"), lax.axis_size("dp")
    my_group, my_dp = lax.axis_index("group"), lax.axis_index("dp")
    group_bits = [1 << i for i in range(n_group.bit_length() - 1)][::-1]
    dp_bits = [1 << i for i in range(n_dp.bit_length() - 1)][::-1]
    sizes = {"dp": n_dp, "group": n_group}
    places = {"dp": my_dp, "group": my_group}
    dp_steps = [("dp", bit) for bit in dp_bits]
    group_steps = [("group", bit) for bit in group_bits]
    far_steps, near_steps = group_steps[:-1], group_steps[-1:]
    wide_first = dp_steps + far_steps + near_steps
    far_first = far_steps + dp_steps + near_steps
    dp_twos, group_twos = (2,) * len(dp_bits), (2,) * len(group_bits)

    def gather_dp(block):
        held = gather_steps(block, dp_steps, sizes, places)
        return held.reshape((n_dp,) + block.shape)

    def gather_group(block):
        held = gather_steps(block, group_steps, sizes, places)
        return held.reshape((n_group,) + block.shape)

    def reduce_dp(blocks):
        return reduce_steps(
            blocks.reshape(dp_twos + blocks.shape[1:]), dp_steps[::-1], sizes, places, dp_steps
        )

    def reduce_group(blocks):
        return reduce_steps(
            blocks.reshape(group_twos + blocks.shape[1:]),
            group_steps[::-1],
            sizes,
            places,
            group_steps,
        )

    def gather_both(block, steps):
        held = gather_steps(block, steps, sizes, places)
        return held.reshape((n_dp, n_group) + block.shape)

    def reduce_both(blocks, steps):
        return reduce_steps(
            blocks.reshape(dp_twos + group_twos + blocks.shape[2:]),
            steps[::-1],
            sizes,
            places,
            dp_steps + group_steps,
        )

    rows = tokens.shape[0]
    width = tokens.shape[1]
    part = width // n_group
    gains = jnp.stack([prenorm_master, midnorm_master]).astype(low)
    gains_all = join_features(gather_group(gains)).astype(jnp.float32)
    gain_first, gain_second = gains_all[0:1], gains_all[1:2]

    query_block = query_master.astype(low).T
    kv_block = jnp.concatenate([key_master_copy.astype(low).T, value_master_copy.astype(low).T], axis=0)
    k_cols = key_master_copy.shape[1]
    w_query_t = gather_both(query_block, wide_first).swapaxes(0, 1).reshape(n_group, width, part)
    kv_blocks = gather_both(kv_block, far_first).swapaxes(0, 1)
    w_kv_t = jnp.concatenate(
        [
            kv_blocks[:, :, :k_cols].reshape(n_group, n_dp * k_cols, part),
            kv_blocks[:, :, k_cols:].reshape(n_group, n_dp * k_cols, part),
        ],
        axis=1,
    )
    w_out_t = gather_both(out_master.astype(low).T, far_first).swapaxes(0, 1)
    w_out_t = w_out_t.reshape(n_group, width, part)

    unit = gate_master.shape[1] // n_group
    unit_rows = n_dp // n_group
    down_cols = down_master.shape[1]
    gate_up_block = jnp.concatenate(
        [
            gate_master.astype(low).T.reshape(n_group, unit, part),
            up_master.astype(low).T.reshape(n_group, unit, part),
        ],
        axis=1,
    )
    down_block = down_master.astype(low).reshape(unit_rows, n_group, unit, down_cols)
    down_block = down_block.transpose(1, 0, 2, 3).reshape(n_group, unit_rows * unit, down_cols)
    gate_up_block = lax.all_to_all(gate_up_block, "group", 0, 0, tiled=True)
    down_block = lax.all_to_all(down_block, "group", 0, 0, tiled=True)
    down_block = down_block.reshape(n_dp * unit, down_cols).T
    w_gate_up = gather_dp(join_features(gate_up_block).reshape(2, unit, width))
    w_gate_t = w_gate_up[:, 0].reshape(n_dp * unit, width)
    w_up_t = w_gate_up[:, 1].reshape(n_dp * unit, width)
    w_down_t = gather_dp(down_block).reshape(width, n_dp * unit)

    cot_held = gather_group(cotangent).reshape(n_group * rows, width)

    sequence_count = rows // SEQUENCE_LENGTH
    heads_per_group = QUERY_HEADS // KEY_VALUE_HEADS
    score_scale = HEAD_SIZE ** (-0.5)
    q_width = QUERY_HEADS * HEAD_SIZE
    k_width = KEY_VALUE_HEADS * HEAD_SIZE
    tok_float = tokens.astype(jnp.float32)
    inv_one = lax.rsqrt(jnp.mean(tok_float * tok_float, axis=-1, keepdims=True) + EPS_NORM)
    scaled_one = tok_float * inv_one
    normed_one = (scaled_one * gain_first).astype(low)
    normed_rel = split_features(normed_one, n_group)

    def project(blocks, weights):
        total = dot(blocks[0], weights[0], 1, 1)
        for r in range(1, n_group):
            total = total + dot(blocks[r], weights[r], 1, 1)
        return total

    query_raw = project(normed_rel, w_query_t)
    kv_raw = project(normed_rel, w_kv_t)
    key_unrotated, value_projected = kv_raw[:, :k_width], kv_raw[:, k_width:]
    cosine_table, sine_table = rotary_tables(SEQUENCE_LENGTH, HEAD_SIZE)
    query_rotated = apply_rotation(
        query_raw.reshape(sequence_count, SEQUENCE_LENGTH, QUERY_HEADS, HEAD_SIZE),
        cosine_table,
        sine_table,
    ).astype(low)
    query_grouped = query_rotated.reshape(
        sequence_count, SEQUENCE_LENGTH, KEY_VALUE_HEADS, heads_per_group, HEAD_SIZE
    )
    key_rotated = apply_rotation(
        key_unrotated.reshape(sequence_count, SEQUENCE_LENGTH, KEY_VALUE_HEADS, HEAD_SIZE),
        cosine_table,
        sine_table,
    ).astype(low)
    value_reduced = value_projected.reshape(
        sequence_count, SEQUENCE_LENGTH, KEY_VALUE_HEADS, HEAD_SIZE
    ).astype(low)
    scores = weighted_values("sqkgd,spkd->skgqp", query_grouped, key_rotated) * score_scale
    causal = jnp.arange(SEQUENCE_LENGTH)[:, None] >= jnp.arange(SEQUENCE_LENGTH)[None, :]
    raw_weights = jnp.where(causal, jnp.exp(scores), 0.0)
    prob_full = raw_weights / jnp.sum(raw_weights, axis=-1, keepdims=True)
    probability_reduced = prob_full.astype(low)
    attended = weighted_values("skgqp,spkd->sqkgd", probability_reduced, value_reduced)
    attended_low = attended.reshape(rows, q_width).astype(low)
    attended_rel = split_features(attended_low, n_group)
    middle = tok_float + project(attended_rel, w_out_t)
    inv_two = lax.rsqrt(jnp.mean(middle * middle, axis=-1, keepdims=True) + EPS_NORM)
    scaled_two = middle * inv_two
    normed_two = (scaled_two * gain_second).astype(low)
    normed_all = gather_group(normed_two).reshape(n_group * rows, width)
    d_hidden = dot(cot_held, w_down_t, 1, 0)
    gate_value = dot(normed_all, w_gate_t, 1, 1)
    up_value = dot(normed_all, w_up_t, 1, 1)
    sigmoid_gate = jax.nn.sigmoid(gate_value)
    silu_gate = gate_value * sigmoid_gate
    hidden = (silu_gate * up_value).astype(low)
    d_gate = (
        d_hidden * up_value * sigmoid_gate * (1.0 + gate_value * (1.0 - sigmoid_gate))
    ).astype(low)
    d_up = (d_hidden * silu_gate).astype(low)
    d_normed_part = dot(d_gate, w_gate_t, 1, 0) + dot(d_up, w_up_t, 1, 0)
    d_normed_two = reduce_group(d_normed_part.astype(low).reshape(n_group, rows, width))

    gate_up_sum = jnp.stack(
        [
            dot(d_gate, normed_all, 0, 0).astype(low).reshape(n_dp, unit, width),
            dot(d_up, normed_all, 0, 0).astype(low).reshape(n_dp, unit, width),
        ],
        axis=1,
    )
    gate_up_sum = reduce_dp(gate_up_sum)
    down_sum = reduce_dp(dot(cot_held, hidden, 0, 0).astype(low).reshape(n_dp, down_cols, n_dp * unit))
    out_part = dot(hidden, w_down_t, 1, 1)
    output = middle + reduce_group(out_part.astype(low).reshape(n_group, rows, width))

    gate_up_back = split_features(gate_up_sum.reshape(2 * unit, width).astype(low), n_group)
    gate_up_back = lax.all_to_all(gate_up_back, "group", 0, 0, tiled=True)
    gate_own = gate_up_back[:, :unit].reshape(n_group * unit, part).T.astype(jnp.float32)
    up_own = gate_up_back[:, unit:].reshape(n_group * unit, part).T.astype(jnp.float32)
    down_back = down_sum.astype(low).T.reshape(n_group, unit_rows * unit, down_cols)
    down_back = lax.all_to_all(down_back, "group", 0, 0, tiled=True)
    down_back = down_back.reshape(n_group, unit_rows, unit, down_cols).transpose(1, 0, 2, 3)
    down_own = down_back.reshape(n_dp * unit, down_cols).astype(jnp.float32)

    cot_float = cotangent.astype(jnp.float32)
    midnorm_sum = jnp.sum(d_normed_two * scaled_two, axis=0, keepdims=True)
    d_scaled_two = d_normed_two * gain_second
    d_middle = cot_float + inv_two * (
        d_scaled_two - scaled_two * jnp.mean(d_scaled_two * scaled_two, axis=-1, keepdims=True)
    )
    d_middle_low = d_middle.astype(low)

    def weight_grad(columns, blocks):
        return jnp.stack([dot(columns, blocks[r], 0, 0).astype(low) for r in range(n_group)])

    def input_part(columns, weights):
        return jnp.stack([dot(columns, weights[r], 1, 0) for r in range(n_group)])

    def by_owner(grads, columns):
        return grads.reshape(n_group, n_dp, columns, part).swapaxes(0, 1)

    out_own = reduce_both(
        by_owner(weight_grad(d_middle_low, attended_rel), width // n_dp), far_first
    ).T
    attended_gradient = join_features(input_part(d_middle_low, w_out_t).astype(low))
    attended_gradient = attended_gradient.reshape(
        sequence_count, SEQUENCE_LENGTH, KEY_VALUE_HEADS, heads_per_group, HEAD_SIZE
    )
    d_prob = weighted_values("sqkgd,spkd->skgqp", attended_gradient, value_reduced)
    inner_sum = jnp.sum(prob_full * d_prob, axis=-1, keepdims=True)
    d_score = (prob_full * (d_prob - inner_sum) * score_scale).astype(low)
    d_query = weighted_values("skgqp,spkd->sqkgd", d_score, key_rotated).reshape(
        sequence_count, SEQUENCE_LENGTH, QUERY_HEADS, HEAD_SIZE
    )
    d_query = inverse_rotation(d_query, cosine_table, sine_table).reshape(rows, q_width).astype(low)
    key_gradient = weighted_values("fceti,ftcel->ficl", d_score, query_grouped)
    key_gradient = (
        inverse_rotation(key_gradient, cosine_table, sine_table).reshape(rows, k_width).astype(low)
    )
    value_gradient = (
        weighted_values("fceti,ftcel->ficl", probability_reduced, attended_gradient)
        .reshape(rows, k_width)
        .astype(low)
    )
    kv_gradient = jnp.concatenate([key_gradient, value_gradient], axis=1)
    query_own = reduce_both(by_owner(weight_grad(d_query, normed_rel), q_width // n_dp), wide_first).T
    kv_sum = jnp.concatenate(
        [
            by_owner(weight_grad(key_gradient, normed_rel), k_cols),
            by_owner(weight_grad(value_gradient, normed_rel), k_cols),
        ],
        axis=2,
    )
    kv_own = reduce_both(kv_sum, far_first)
    key_own, value_own = kv_own[:k_cols].T, kv_own[k_cols:].T
    d_normed_blocks = input_part(d_query, w_query_t) + input_part(kv_gradient, w_kv_t)
    d_normed_one = join_features(d_normed_blocks)
    prenorm_sum = jnp.sum(d_normed_one * scaled_one, axis=0, keepdims=True)
    d_scaled_one = d_normed_one * gain_first
    input_grad = d_middle + inv_one * (
        d_scaled_one - scaled_one * jnp.mean(d_scaled_one * scaled_one, axis=-1, keepdims=True)
    )

    gain_rows = jnp.concatenate([prenorm_sum, midnorm_sum], axis=0)
    gain_rel = split_features(gain_rows, n_group)
    gain_own = reduce_group(gain_rel)
    for bit in dp_bits:
        mine = gain_own.astype(low)
        gain_own = mine.astype(jnp.float32) + swap(mine, "dp", bit, n_dp).astype(jnp.float32)
    prenorm_own, midnorm_own = gain_own[0], gain_own[1]

    owned = (
        prenorm_own,
        query_own,
        key_own,
        value_own,
        out_own,
        midnorm_own,
        gate_own,
        up_own,
        down_own,
    )
    mean_list = (
        prenorm_mean,
        query_mean,
        key_first_moment,
        value_first_moment,
        out_mean,
        midnorm_mean,
        gate_mean,
        up_mean,
        down_mean,
    )
    square_list = (
        prenorm_square,
        query_square,
        key_second_moment,
        value_second_moment,
        out_square,
        midnorm_square,
        gate_square,
        up_square,
        down_square,
    )
    rate_list = (
        RATE_GAIN,
        RATE_MATRIX,
        RATE_MATRIX,
        RATE_MATRIX,
        RATE_OUTPUT,
        RATE_GAIN,
        RATE_MATRIX,
        RATE_MATRIX,
        RATE_MATRIX,
    )
    decays = (
        0.0,
        DECAY_RATE,
        DECAY_RATE,
        DECAY_RATE,
        DECAY_RATE,
        0.0,
        DECAY_RATE,
        DECAY_RATE,
        DECAY_RATE,
    )
    results = [
        adam_update(masters[k], mean_list[k], square_list[k], owned[k], rate_list[k], decays[k])
        for k in range(9)
    ]
    return (
        output,
        input_grad,
        owned[0],
        owned[1],
        owned[2],
        owned[3],
        owned[4],
        owned[5],
        owned[6],
        owned[7],
        owned[8],
        results[0][0],
        results[1][0],
        results[2][0],
        results[3][0],
        results[4][0],
        results[5][0],
        results[6][0],
        results[7][0],
        results[8][0],
        results[0][1],
        results[1][1],
        results[2][1],
        results[3][1],
        results[4][1],
        results[5][1],
        results[6][1],
        results[7][1],
        results[8][1],
        results[0][2],
        results[1][2],
        results[2][2],
        results[3][2],
        results[4][2],
        results[5][2],
        results[6][2],
        results[7][2],
        results[8][2],
    )


def solution(mesh):
    placed = (
        P(("dp", "group"), None),
        P(("dp", "group"), None),
        P("group"),
        P("group", "dp"),
        P("group", "dp"),
        P("group", "dp"),
        P("group", "dp"),
        P("group"),
        P("group", "dp"),
        P("group", "dp"),
        P("group", "dp"),
        P("group"),
        P("group", "dp"),
        P("group", "dp"),
        P("group", "dp"),
        P("group", "dp"),
        P("group"),
        P("group", "dp"),
        P("group", "dp"),
        P("group", "dp"),
        P("group"),
        P("group", "dp"),
        P("group", "dp"),
        P("group", "dp"),
        P("group", "dp"),
        P("group"),
        P("group", "dp"),
        P("group", "dp"),
        P("group", "dp"),
    )
    return jax.shard_map(
        per_device,
        mesh=mesh,
        in_specs=placed,
        out_specs=(
            P(("dp", "group"), None),
            P(("dp", "group"), None),
            P("group"),
            P("group", "dp"),
            P("group", "dp"),
            P("group", "dp"),
            P("group", "dp"),
            P("group"),
            P("group", "dp"),
            P("group", "dp"),
            P("group", "dp"),
            P("group"),
            P("group", "dp"),
            P("group", "dp"),
            P("group", "dp"),
            P("group", "dp"),
            P("group"),
            P("group", "dp"),
            P("group", "dp"),
            P("group", "dp"),
            P("group"),
            P("group", "dp"),
            P("group", "dp"),
            P("group", "dp"),
            P("group", "dp"),
            P("group"),
            P("group", "dp"),
            P("group", "dp"),
            P("group", "dp"),
            P("group"),
            P("group", "dp"),
            P("group", "dp"),
            P("group", "dp"),
            P("group", "dp"),
            P("group"),
            P("group", "dp"),
            P("group", "dp"),
            P("group", "dp"),
        ),
        check_vma=False,
    )
```

```python
import jax
import jax.numpy as jnp
from jax import lax
from jax.experimental import pallas as pl
from jax.experimental.pallas import tpu as pltpu
from jax.sharding import PartitionSpec as P

QUERY_HEADS = 15
KEY_VALUE_HEADS = 5
HEAD_SIZE = 64
SEQUENCE_LENGTH = 128


EPS_NORM = 1e-05
BETA_ONE = 0.9
BETA_TWO = 0.95
ADAM_EPS = 1e-08
RATE_MATRIX = 0.015
RATE_OUTPUT = 0.05
RATE_GAIN = 0.4
DECAY_RATE = 0.1
ADAM_STEP = 4.0
ROPE_BASE = 10000.0


def weighted_values(pattern, left_op, right_op):
    return jnp.einsum(pattern, left_op, right_op, preferred_element_type=jnp.float32)


def rotary_tables(length, head_dim):
    half_dim = head_dim // 2
    frequency = ROPE_BASE ** (-(jnp.arange(half_dim, dtype=jnp.float32) * 2.0 / head_dim))
    angles = jnp.arange(length, dtype=jnp.float32)[:, None] * frequency[None, :]
    return (jnp.cos(angles), jnp.sin(angles))


def apply_rotation(values, cosine_table, sine_table):
    half_dim = values.shape[-1] // 2
    first_half = values[..., :half_dim]
    second = values[..., half_dim:]
    cos_part = cosine_table[:, None, :]
    sin_part = sine_table[:, None, :]
    return jnp.concatenate(
        [first_half * cos_part - second * sin_part, second * cos_part + first_half * sin_part],
        axis=-1,
    )


def inverse_rotation(values, cosine_table, sine_table):
    half_dim = values.shape[-1] // 2
    first_half = values[..., :half_dim]
    second = values[..., half_dim:]
    cos_part = cosine_table[:, None, :]
    sin_part = sine_table[:, None, :]
    return jnp.concatenate(
        [first_half * cos_part + second * sin_part, second * cos_part - first_half * sin_part],
        axis=-1,
    )


def swap(value, axis, bit, size):
    return lax.ppermute(value, axis, [(i, i ^ bit) for i in range(size)])


def gather_steps(value, steps, sizes, places):
    held, done = value, []
    for axis, bit in steps:
        got = swap(held, axis, bit, sizes[axis])
        upper = (places[axis] & bit) != 0
        at = len([d for d in done if (d[0] == "dp" and axis == "group") or (d[0] == axis and d[1] > bit)])
        low_part, high_part = jnp.where(upper, got, held), jnp.where(upper, held, got)
        held = jnp.stack([low_part, high_part], axis=at)
        done = done + [(axis, bit)]
    return held


def reduce_steps(value, steps, sizes, places, done, after=()):
    held, done = value, list(done)
    after = list(after) + [None] * (len(steps) - len(after))
    for (axis, bit), behind in zip(steps, after):
        at = done.index((axis, bit))
        mine = ((places[axis] & bit) != 0).astype(jnp.int32)
        sent = lax.dynamic_index_in_dim(held, 1 - mine, at, keepdims=False).astype(jnp.bfloat16)
        kept = lax.dynamic_index_in_dim(held, mine, at, keepdims=False)
        got = swap(sent, axis, bit, sizes[axis])
        if behind is not None:
            got, _ = lax.optimization_barrier((got, behind))
        held = (kept.astype(jnp.float32) + got.astype(jnp.float32)).astype(jnp.bfloat16)
        done.pop(at)
        last = kept.astype(jnp.float32) + got.astype(jnp.float32)
    return last


def dot(left_op, right_op, left_dim, right_dim):
    return lax.dot_general(
        left_op, right_op, (((left_dim,), (right_dim,)), ((), ())), preferred_element_type=jnp.float32
    )


def mix_kernel(normed_ref, cot_ref, gate_ref, up_ref, down_ref, d_normed_ref, hidden_ref, dg_ref, du_ref):
    normed = normed_ref[...]
    gate_value = dot(normed, gate_ref[...], 1, 1)
    up_value = dot(normed, up_ref[...], 1, 1)
    d_hidden = dot(cot_ref[...], down_ref[...], 1, 0)
    sigmoid_gate = jax.nn.sigmoid(gate_value)
    silu_gate = gate_value * sigmoid_gate
    hidden_ref[...] = (silu_gate * up_value).astype(jnp.bfloat16)
    d_gate = (
        d_hidden * up_value * sigmoid_gate * (1.0 + gate_value * (1.0 - sigmoid_gate))
    ).astype(jnp.bfloat16)
    d_up = (d_hidden * silu_gate).astype(jnp.bfloat16)
    dg_ref[...] = d_gate
    du_ref[...] = d_up
    d_normed = dot(d_gate, gate_ref[...], 1, 0) + dot(d_up, up_ref[...], 1, 0)
    d_normed_ref[...] = d_normed.astype(jnp.bfloat16)


def feed_forward(normed, cot, w_gate_t, w_up_t, w_down_t):
    count, width = normed.shape
    units = w_gate_t.shape[0]
    step = 256
    whole = lambda shape: pl.BlockSpec(shape, lambda i: (0, 0))
    rows = lambda cols: pl.BlockSpec((step, cols), lambda i: (i, 0))
    shape = lambda cols: jax.ShapeDtypeStruct((count, cols), jnp.bfloat16)
    return pl.pallas_call(
        mix_kernel,
        grid=(count // step,),
        in_specs=[
            rows(width),
            rows(width),
            whole((units, width)),
            whole((units, width)),
            whole((width, units)),
        ],
        out_specs=[rows(width), rows(units), rows(units), rows(units)],
        out_shape=[shape(width), shape(units), shape(units), shape(units)],
        compiler_params=pltpu.CompilerParams(vmem_limit_bytes=56 << 20),
        cost_estimate=pl.CostEstimate(
            flops=10 * count * units * width, transcendentals=count * units, bytes_accessed=12 << 20
        ),
        name="feed_forward",
    )(normed, cot, w_gate_t, w_up_t, w_down_t)


def grad_kernel(normed_ref, cot_ref, hidden_ref, dg_ref, du_ref, gate_ref, up_ref, down_ref):
    gate_ref[...] = dot(dg_ref[...], normed_ref[...], 0, 0).astype(jnp.bfloat16)
    up_ref[...] = dot(du_ref[...], normed_ref[...], 0, 0).astype(jnp.bfloat16)
    down_ref[...] = dot(cot_ref[...], hidden_ref[...], 0, 0).astype(jnp.bfloat16)


def feed_forward_grads(normed, cot, hidden, d_gate, d_up):
    count, width = normed.shape
    units = hidden.shape[1]
    vmem = pl.BlockSpec(memory_space=pltpu.VMEM)
    return pl.pallas_call(
        grad_kernel,
        in_specs=[vmem] * 5,
        out_specs=[vmem] * 3,
        out_shape=[
            jax.ShapeDtypeStruct((units, width), jnp.bfloat16),
            jax.ShapeDtypeStruct((units, width), jnp.bfloat16),
            jax.ShapeDtypeStruct((width, units), jnp.bfloat16),
        ],
        compiler_params=pltpu.CompilerParams(vmem_limit_bytes=56 << 20),
        cost_estimate=pl.CostEstimate(
            flops=6 * count * units * width, transcendentals=0, bytes_accessed=8 << 20
        ),
        name="feed_forward_grads",
    )(normed, cot, hidden, d_gate, d_up)


def split_features(values, parts):
    width = values.shape[1] // parts
    return jnp.stack([values[:, i * width : (i + 1) * width] for i in range(parts)])


def join_features(blocks):
    return jnp.concatenate([blocks[i] for i in range(blocks.shape[0])], axis=1)


def adam_update(master, mean_old, square_old, gradient, rate, decay):
    momentum = BETA_ONE * mean_old + (1.0 - BETA_ONE) * gradient
    variance = BETA_TWO * square_old + (1.0 - BETA_TWO) * gradient * gradient
    fix_one = 1.0 - BETA_ONE**ADAM_STEP
    fix_two = 1.0 - BETA_TWO**ADAM_STEP
    update = momentum / fix_one / (jnp.sqrt(variance / fix_two) + ADAM_EPS) + decay * master
    return (master - rate * update, momentum, variance)


def per_device(
    tokens,
    cotangent,
    prenorm_master,
    query_master,
    key_master_copy,
    value_master_copy,
    out_master,
    midnorm_master,
    gate_master,
    up_master,
    down_master,
    prenorm_mean,
    query_mean,
    key_first_moment,
    value_first_moment,
    out_mean,
    midnorm_mean,
    gate_mean,
    up_mean,
    down_mean,
    prenorm_square,
    query_square,
    key_second_moment,
    value_second_moment,
    out_square,
    midnorm_square,
    gate_square,
    up_square,
    down_square,
):
    masters = (
        prenorm_master,
        query_master,
        key_master_copy,
        value_master_copy,
        out_master,
        midnorm_master,
        gate_master,
        up_master,
        down_master,
    )
    low = jnp.bfloat16
    n_group, n_dp = lax.axis_size("group"), lax.axis_size("dp")
    my_group, my_dp = lax.axis_index("group"), lax.axis_index("dp")
    group_bits = [1 << i for i in range(n_group.bit_length() - 1)][::-1]
    dp_bits = [1 << i for i in range(n_dp.bit_length() - 1)][::-1]
    sizes = {"dp": n_dp, "group": n_group}
    places = {"dp": my_dp, "group": my_group}
    dp_steps = [("dp", bit) for bit in dp_bits]
    group_steps = [("group", bit) for bit in group_bits]
    far_steps, near_steps = group_steps[:-1], group_steps[-1:]
    wide_first = dp_steps + far_steps + near_steps
    far_first = far_steps + dp_steps + near_steps
    dp_twos, group_twos = (2,) * len(dp_bits), (2,) * len(group_bits)

    def gather_dp(block):
        held = gather_steps(block, dp_steps, sizes, places)
        return held.reshape((n_dp,) + block.shape)

    def gather_group(block):
        held = gather_steps(block, group_steps, sizes, places)
        return held.reshape((n_group,) + block.shape)

    def reduce_dp(blocks):
        return reduce_steps(
            blocks.reshape(dp_twos + blocks.shape[1:]), dp_steps[::-1], sizes, places, dp_steps
        )

    def reduce_group(blocks):
        return reduce_steps(
            blocks.reshape(group_twos + blocks.shape[1:]),
            group_steps[::-1],
            sizes,
            places,
            group_steps,
        )

    def gather_both(block, steps):
        held = gather_steps(block, steps, sizes, places)
        return held.reshape((n_dp, n_group) + block.shape)

    def reduce_both(blocks, steps):
        return reduce_steps(
            blocks.reshape(dp_twos + group_twos + blocks.shape[2:]),
            steps[::-1],
            sizes,
            places,
            dp_steps + group_steps,
        )

    rows = tokens.shape[0]
    width = tokens.shape[1]
    part = width // n_group
    gains = jnp.stack([prenorm_master, midnorm_master]).astype(low)
    gains_all = join_features(gather_group(gains)).astype(jnp.float32)
    gain_first, gain_second = gains_all[0:1], gains_all[1:2]

    query_block = query_master.astype(low).T
    kv_block = jnp.concatenate([key_master_copy.astype(low).T, value_master_copy.astype(low).T], axis=0)
    k_cols = key_master_copy.shape[1]
    w_query_t = gather_both(query_block, wide_first).swapaxes(0, 1).reshape(n_group, width, part)
    kv_blocks = gather_both(kv_block, far_first).swapaxes(0, 1)
    w_kv_t = jnp.concatenate(
        [
            kv_blocks[:, :, :k_cols].reshape(n_group, n_dp * k_cols, part),
            kv_blocks[:, :, k_cols:].reshape(n_group, n_dp * k_cols, part),
        ],
        axis=1,
    )
    w_out_t = gather_both(out_master.astype(low).T, far_first).swapaxes(0, 1)
    w_out_t = w_out_t.reshape(n_group, width, part)

    unit = gate_master.shape[1] // n_group
    unit_rows = n_dp // n_group
    down_cols = down_master.shape[1]
    gate_up_block = jnp.concatenate(
        [
            gate_master.astype(low).T.reshape(n_group, unit, part),
            up_master.astype(low).T.reshape(n_group, unit, part),
        ],
        axis=1,
    )
    down_block = down_master.astype(low).reshape(unit_rows, n_group, unit, down_cols)
    down_block = down_block.transpose(1, 0, 2, 3).reshape(n_group, unit_rows * unit, down_cols)
    gate_up_block = lax.all_to_all(gate_up_block, "group", 0, 0, tiled=True)
    down_block = lax.all_to_all(down_block, "group", 0, 0, tiled=True)
    down_block = down_block.reshape(n_dp * unit, down_cols).T
    gate_up_block = join_features(gate_up_block)
    w_gate_t = gather_dp(gate_up_block[:unit]).reshape(n_dp * unit, width)
    w_up_t = gather_dp(gate_up_block[unit:]).reshape(n_dp * unit, width)
    w_down_t = gather_dp(down_block).reshape(width, n_dp * unit)

    cot_held = gather_group(cotangent).reshape(n_group * rows, width)

    sequence_count = rows // SEQUENCE_LENGTH
    heads_per_group = QUERY_HEADS // KEY_VALUE_HEADS
    score_scale = HEAD_SIZE ** (-0.5)
    q_width = QUERY_HEADS * HEAD_SIZE
    k_width = KEY_VALUE_HEADS * HEAD_SIZE
    tok_float = tokens.astype(jnp.float32)
    inv_one = lax.rsqrt(jnp.mean(tok_float * tok_float, axis=-1, keepdims=True) + EPS_NORM)
    scaled_one = tok_float * inv_one
    normed_one = (scaled_one * gain_first).astype(low)
    normed_rel = split_features(normed_one, n_group)

    def project(blocks, weights):
        total = dot(blocks[0], weights[0], 1, 1)
        for r in range(1, n_group):
            total = total + dot(blocks[r], weights[r], 1, 1)
        return total

    query_raw = project(normed_rel, w_query_t)
    kv_raw = project(normed_rel, w_kv_t)
    key_unrotated, value_projected = kv_raw[:, :k_width], kv_raw[:, k_width:]
    cosine_table, sine_table = rotary_tables(SEQUENCE_LENGTH, HEAD_SIZE)
    query_rotated = apply_rotation(
        query_raw.reshape(sequence_count, SEQUENCE_LENGTH, QUERY_HEADS, HEAD_SIZE),
        cosine_table,
        sine_table,
    ).astype(low)
    query_grouped = query_rotated.reshape(
        sequence_count, SEQUENCE_LENGTH, KEY_VALUE_HEADS, heads_per_group, HEAD_SIZE
    )
    key_rotated = apply_rotation(
        key_unrotated.reshape(sequence_count, SEQUENCE_LENGTH, KEY_VALUE_HEADS, HEAD_SIZE),
        cosine_table,
        sine_table,
    ).astype(low)
    value_reduced = value_projected.reshape(
        sequence_count, SEQUENCE_LENGTH, KEY_VALUE_HEADS, HEAD_SIZE
    ).astype(low)
    scores = weighted_values("sqkgd,spkd->skgqp", query_grouped, key_rotated) * score_scale
    causal = jnp.arange(SEQUENCE_LENGTH)[:, None] >= jnp.arange(SEQUENCE_LENGTH)[None, :]
    raw_weights = jnp.where(causal, jnp.exp(scores), 0.0)
    prob_full = raw_weights / jnp.sum(raw_weights, axis=-1, keepdims=True)
    probability_reduced = prob_full.astype(low)
    attended = weighted_values("skgqp,spkd->sqkgd", probability_reduced, value_reduced)
    attended_low = attended.reshape(rows, q_width).astype(low)
    attended_rel = split_features(attended_low, n_group)
    middle = tok_float + project(attended_rel, w_out_t)
    inv_two = lax.rsqrt(jnp.mean(middle * middle, axis=-1, keepdims=True) + EPS_NORM)
    scaled_two = middle * inv_two
    normed_two = (scaled_two * gain_second).astype(low)
    normed_all = gather_group(normed_two).reshape(n_group * rows, width)
    d_normed_part, hidden, d_gate, d_up = feed_forward(
        normed_all, cot_held, w_gate_t, w_up_t, w_down_t
    )
    d_normed_two = reduce_group(d_normed_part.reshape(n_group, rows, width))

    cot_float = cotangent.astype(jnp.float32)
    midnorm_sum = jnp.sum(d_normed_two * scaled_two, axis=0, keepdims=True)
    d_scaled_two = d_normed_two * gain_second
    d_middle = cot_float + inv_two * (
        d_scaled_two - scaled_two * jnp.mean(d_scaled_two * scaled_two, axis=-1, keepdims=True)
    )
    d_middle_low = d_middle.astype(low)

    def weight_grad(columns, blocks):
        return jnp.stack([dot(columns, blocks[r], 0, 0).astype(low) for r in range(n_group)])

    def input_part(columns, weights):
        return jnp.stack([dot(columns, weights[r], 1, 0) for r in range(n_group)])

    def by_owner(grads, columns):
        return grads.reshape(n_group, n_dp, columns, part).swapaxes(0, 1)

    out_own = reduce_both(
        by_owner(weight_grad(d_middle_low, attended_rel), width // n_dp), wide_first
    ).T
    attended_gradient = join_features(input_part(d_middle_low, w_out_t).astype(low))
    attended_gradient = attended_gradient.reshape(
        sequence_count, SEQUENCE_LENGTH, KEY_VALUE_HEADS, heads_per_group, HEAD_SIZE
    )
    d_prob = weighted_values("sqkgd,spkd->skgqp", attended_gradient, value_reduced)
    inner_sum = jnp.sum(prob_full * d_prob, axis=-1, keepdims=True)
    d_score = (prob_full * (d_prob - inner_sum) * score_scale).astype(low)
    d_query = weighted_values("skgqp,spkd->sqkgd", d_score, key_rotated).reshape(
        sequence_count, SEQUENCE_LENGTH, QUERY_HEADS, HEAD_SIZE
    )
    d_query = inverse_rotation(d_query, cosine_table, sine_table).reshape(rows, q_width).astype(low)
    key_gradient = weighted_values("fceti,ftcel->ficl", d_score, query_grouped)
    key_gradient = (
        inverse_rotation(key_gradient, cosine_table, sine_table).reshape(rows, k_width).astype(low)
    )
    value_gradient = (
        weighted_values("fceti,ftcel->ficl", probability_reduced, attended_gradient)
        .reshape(rows, k_width)
        .astype(low)
    )
    gate_grad, up_grad, down_grad = feed_forward_grads(normed_all, cot_held, hidden, d_gate, d_up)

    def reduce_units(grads, steps, after):
        blocks = grads.reshape(dp_twos + (grads.shape[0] // n_dp, grads.shape[1]))
        return reduce_steps(blocks, steps, sizes, places, dp_steps, after)

    gate_sum = reduce_units(gate_grad, dp_steps[::-1], (d_score, key_gradient))
    up_sum = reduce_units(up_grad, dp_steps[::-1], (d_score, key_gradient))
    down_sum = reduce_units(down_grad, dp_steps[-2:-1] + dp_steps[:-2] + dp_steps[-1:], (d_middle_low, d_score))
    gate_up_sum = jnp.concatenate([gate_sum, up_sum], axis=0)
    out_part = dot(hidden, w_down_t, 1, 1)
    output = middle + reduce_group(out_part.astype(low).reshape(n_group, rows, width))

    gate_up_back = split_features(gate_up_sum.astype(low), n_group)
    gate_up_back = lax.all_to_all(gate_up_back, "group", 0, 0, tiled=True)
    gate_own = gate_up_back[:, :unit].reshape(n_group * unit, part).T.astype(jnp.float32)
    up_own = gate_up_back[:, unit:].reshape(n_group * unit, part).T.astype(jnp.float32)
    down_back = down_sum.astype(low).T.reshape(n_group, unit_rows * unit, down_cols)
    down_back = lax.all_to_all(down_back, "group", 0, 0, tiled=True)
    down_back = down_back.reshape(n_group, unit_rows, unit, down_cols).transpose(1, 0, 2, 3)
    down_own = down_back.reshape(n_dp * unit, down_cols).astype(jnp.float32)

    kv_gradient = jnp.concatenate([key_gradient, value_gradient], axis=1)
    query_own = reduce_both(by_owner(weight_grad(d_query, normed_rel), q_width // n_dp), wide_first).T
    kv_sum = jnp.concatenate(
        [
            by_owner(weight_grad(key_gradient, normed_rel), k_cols),
            by_owner(weight_grad(value_gradient, normed_rel), k_cols),
        ],
        axis=2,
    )
    kv_own = reduce_both(kv_sum, far_first)
    key_own, value_own = kv_own[:k_cols].T, kv_own[k_cols:].T
    d_normed_blocks = input_part(d_query, w_query_t) + input_part(kv_gradient, w_kv_t)
    d_normed_one = join_features(d_normed_blocks)
    prenorm_sum = jnp.sum(d_normed_one * scaled_one, axis=0, keepdims=True)
    d_scaled_one = d_normed_one * gain_first
    input_grad = d_middle + inv_one * (
        d_scaled_one - scaled_one * jnp.mean(d_scaled_one * scaled_one, axis=-1, keepdims=True)
    )

    gain_rows = jnp.concatenate([prenorm_sum, midnorm_sum], axis=0)
    gain_rel = split_features(gain_rows, n_group)
    gain_own = reduce_group(gain_rel)
    for bit in dp_bits:
        mine = gain_own.astype(low)
        gain_own = mine.astype(jnp.float32) + swap(mine, "dp", bit, n_dp).astype(jnp.float32)
    prenorm_own, midnorm_own = gain_own[0], gain_own[1]

    owned = (
        prenorm_own,
        query_own,
        key_own,
        value_own,
        out_own,
        midnorm_own,
        gate_own,
        up_own,
        down_own,
    )
    mean_list = (
        prenorm_mean,
        query_mean,
        key_first_moment,
        value_first_moment,
        out_mean,
        midnorm_mean,
        gate_mean,
        up_mean,
        down_mean,
    )
    square_list = (
        prenorm_square,
        query_square,
        key_second_moment,
        value_second_moment,
        out_square,
        midnorm_square,
        gate_square,
        up_square,
        down_square,
    )
    rate_list = (
        RATE_GAIN,
        RATE_MATRIX,
        RATE_MATRIX,
        RATE_MATRIX,
        RATE_OUTPUT,
        RATE_GAIN,
        RATE_MATRIX,
        RATE_MATRIX,
        RATE_MATRIX,
    )
    decays = (
        0.0,
        DECAY_RATE,
        DECAY_RATE,
        DECAY_RATE,
        DECAY_RATE,
        0.0,
        DECAY_RATE,
        DECAY_RATE,
        DECAY_RATE,
    )
    results = [
        adam_update(masters[k], mean_list[k], square_list[k], owned[k], rate_list[k], decays[k])
        for k in range(9)
    ]
    return (
        output,
        input_grad,
        owned[0],
        owned[1],
        owned[2],
        owned[3],
        owned[4],
        owned[5],
        owned[6],
        owned[7],
        owned[8],
        results[0][0],
        results[1][0],
        results[2][0],
        results[3][0],
        results[4][0],
        results[5][0],
        results[6][0],
        results[7][0],
        results[8][0],
        results[0][1],
        results[1][1],
        results[2][1],
        results[3][1],
        results[4][1],
        results[5][1],
        results[6][1],
        results[7][1],
        results[8][1],
        results[0][2],
        results[1][2],
        results[2][2],
        results[3][2],
        results[4][2],
        results[5][2],
        results[6][2],
        results[7][2],
        results[8][2],
    )


def solution(mesh):
    placed = (
        P(("dp", "group"), None),
        P(("dp", "group"), None),
        P("group"),
        P("group", "dp"),
        P("group", "dp"),
        P("group", "dp"),
        P("group", "dp"),
        P("group"),
        P("group", "dp"),
        P("group", "dp"),
        P("group", "dp"),
        P("group"),
        P("group", "dp"),
        P("group", "dp"),
        P("group", "dp"),
        P("group", "dp"),
        P("group"),
        P("group", "dp"),
        P("group", "dp"),
        P("group", "dp"),
        P("group"),
        P("group", "dp"),
        P("group", "dp"),
        P("group", "dp"),
        P("group", "dp"),
        P("group"),
        P("group", "dp"),
        P("group", "dp"),
        P("group", "dp"),
    )
    return jax.shard_map(
        per_device,
        mesh=mesh,
        in_specs=placed,
        out_specs=(
            P(("dp", "group"), None),
            P(("dp", "group"), None),
            P("group"),
            P("group", "dp"),
            P("group", "dp"),
            P("group", "dp"),
            P("group", "dp"),
            P("group"),
            P("group", "dp"),
            P("group", "dp"),
            P("group", "dp"),
            P("group"),
            P("group", "dp"),
            P("group", "dp"),
            P("group", "dp"),
            P("group", "dp"),
            P("group"),
            P("group", "dp"),
            P("group", "dp"),
            P("group", "dp"),
            P("group"),
            P("group", "dp"),
            P("group", "dp"),
            P("group", "dp"),
            P("group", "dp"),
            P("group"),
            P("group", "dp"),
            P("group", "dp"),
            P("group", "dp"),
            P("group"),
            P("group", "dp"),
            P("group", "dp"),
            P("group", "dp"),
            P("group", "dp"),
            P("group"),
            P("group", "dp"),
            P("group", "dp"),
            P("group", "dp"),
        ),
        check_vma=False,
    )
```

```python
import jax
import jax.numpy as jnp
from jax import lax
from jax.experimental import pallas as pl
from jax.experimental.pallas import tpu as pltpu
from jax.sharding import PartitionSpec as P

QUERY_HEADS = 15
KEY_VALUE_HEADS = 5
HEAD_SIZE = 64
SEQUENCE_LENGTH = 128


EPS_NORM = 1e-05
BETA_ONE = 0.9
BETA_TWO = 0.95
ADAM_EPS = 1e-08
RATE_MATRIX = 0.015
RATE_OUTPUT = 0.05
RATE_GAIN = 0.4
DECAY_RATE = 0.1
ADAM_STEP = 4.0
ROPE_BASE = 10000.0


def weighted_values(pattern, left_op, right_op):
    return jnp.einsum(pattern, left_op, right_op, preferred_element_type=jnp.float32)


def rotary_tables(length, head_dim):
    half_dim = head_dim // 2
    frequency = ROPE_BASE ** (-(jnp.arange(half_dim, dtype=jnp.float32) * 2.0 / head_dim))
    angles = jnp.arange(length, dtype=jnp.float32)[:, None] * frequency[None, :]
    return (jnp.cos(angles), jnp.sin(angles))


def apply_rotation(values, cosine_table, sine_table):
    half_dim = values.shape[-1] // 2
    first_half = values[..., :half_dim]
    second = values[..., half_dim:]
    cos_part = cosine_table[:, None, :]
    sin_part = sine_table[:, None, :]
    return jnp.concatenate(
        [first_half * cos_part - second * sin_part, second * cos_part + first_half * sin_part],
        axis=-1,
    )


def inverse_rotation(values, cosine_table, sine_table):
    half_dim = values.shape[-1] // 2
    first_half = values[..., :half_dim]
    second = values[..., half_dim:]
    cos_part = cosine_table[:, None, :]
    sin_part = sine_table[:, None, :]
    return jnp.concatenate(
        [first_half * cos_part + second * sin_part, second * cos_part - first_half * sin_part],
        axis=-1,
    )


def swap(value, axis, bit, size):
    return lax.ppermute(value, axis, [(i, i ^ bit) for i in range(size)])


def gather_steps(value, steps, sizes, places):
    held, done = value, []
    for axis, bit in steps:
        got = swap(held, axis, bit, sizes[axis])
        upper = (places[axis] & bit) != 0
        at = len([d for d in done if (d[0] == "dp" and axis == "group") or (d[0] == axis and d[1] > bit)])
        low_part, high_part = jnp.where(upper, got, held), jnp.where(upper, held, got)
        held = jnp.stack([low_part, high_part], axis=at)
        done = done + [(axis, bit)]
    return held


class Chain:
    def __init__(self, held, steps, done, sizes, places):
        self.held, self.steps, self.done = held, list(steps), list(done)
        self.sizes, self.places = sizes, places

    def start(self):
        axis, bit = self.steps.pop(0)
        if (axis, bit) in self.done:
            at = self.done.index((axis, bit))
            mine = ((self.places[axis] & bit) != 0).astype(jnp.int32)
            sent = lax.dynamic_index_in_dim(self.held, 1 - mine, at, keepdims=False)
            self.kept = lax.dynamic_index_in_dim(self.held, mine, at, keepdims=False)
            self.done.pop(at)
        else:
            sent = self.kept = self.held
        return swap(sent, axis, bit, self.sizes[axis])

    def finish(self, got):
        self.total = self.kept.astype(jnp.float32) + got.astype(jnp.float32)
        self.held = self.total.astype(jnp.bfloat16)


class TokenChain(Chain):
    def start(self):
        axis, bit = self.steps.pop(0)
        half = self.held.shape[0] // 2
        self.kept = self.held[:half]
        return swap(self.held[half:], axis, bit, self.sizes[axis])


def start_all(chains):
    return tuple(chain.start() for chain in chains)


def finish_all(chains, gots, behind=()):
    gots = lax.optimization_barrier(tuple(gots) + tuple(behind))[: len(gots)]
    for chain, got in zip(chains, gots):
        chain.finish(got)
    return gots


def dot(left_op, right_op, left_dim, right_dim):
    return lax.dot_general(
        left_op, right_op, (((left_dim,), (right_dim,)), ((), ())), preferred_element_type=jnp.float32
    )


def mix_kernel(normed_ref, cot_ref, gate_ref, up_ref, down_ref, d_normed_ref, hidden_ref, dg_ref, du_ref):
    normed = normed_ref[...]
    gate_value = dot(normed, gate_ref[...], 1, 1)
    up_value = dot(normed, up_ref[...], 1, 1)
    d_hidden = dot(cot_ref[...], down_ref[...], 1, 0)
    sigmoid_gate = jax.nn.sigmoid(gate_value)
    silu_gate = gate_value * sigmoid_gate
    hidden_ref[...] = (silu_gate * up_value).astype(jnp.bfloat16)
    d_gate = (
        d_hidden * up_value * sigmoid_gate * (1.0 + gate_value * (1.0 - sigmoid_gate))
    ).astype(jnp.bfloat16)
    d_up = (d_hidden * silu_gate).astype(jnp.bfloat16)
    dg_ref[...] = d_gate
    du_ref[...] = d_up
    d_normed = dot(d_gate, gate_ref[...], 1, 0) + dot(d_up, up_ref[...], 1, 0)
    d_normed_ref[...] = d_normed.astype(jnp.bfloat16)


def feed_forward(normed, cot, w_gate_t, w_up_t, w_down_t):
    count, width = normed.shape
    units = w_gate_t.shape[0]
    step = 256
    whole = lambda shape: pl.BlockSpec(shape, lambda i: (0, 0))
    rows = lambda cols: pl.BlockSpec((step, cols), lambda i: (i, 0))
    shape = lambda cols: jax.ShapeDtypeStruct((count, cols), jnp.bfloat16)
    return pl.pallas_call(
        mix_kernel,
        grid=(count // step,),
        in_specs=[
            rows(width),
            rows(width),
            whole((units, width)),
            whole((units, width)),
            whole((width, units)),
        ],
        out_specs=[rows(width), rows(units), rows(units), rows(units)],
        out_shape=[shape(width), shape(units), shape(units), shape(units)],
        compiler_params=pltpu.CompilerParams(vmem_limit_bytes=56 << 20),
        cost_estimate=pl.CostEstimate(
            flops=10 * count * units * width, transcendentals=count * units, bytes_accessed=12 << 20
        ),
        name="feed_forward",
    )(normed, cot, w_gate_t, w_up_t, w_down_t)


def grad_kernel(normed_ref, cot_ref, hidden_ref, dg_ref, du_ref, gate_ref, up_ref, down_ref):
    gate_ref[...] = dot(dg_ref[...], normed_ref[...], 0, 0).astype(jnp.bfloat16)
    up_ref[...] = dot(du_ref[...], normed_ref[...], 0, 0).astype(jnp.bfloat16)
    down_ref[...] = dot(cot_ref[...], hidden_ref[...], 0, 0).astype(jnp.bfloat16)


def feed_forward_grads(normed, cot, hidden, d_gate, d_up):
    count, width = normed.shape
    units = hidden.shape[1]
    vmem = pl.BlockSpec(memory_space=pltpu.VMEM)
    return pl.pallas_call(
        grad_kernel,
        in_specs=[vmem] * 5,
        out_specs=[vmem] * 3,
        out_shape=[
            jax.ShapeDtypeStruct((units, width), jnp.bfloat16),
            jax.ShapeDtypeStruct((units, width), jnp.bfloat16),
            jax.ShapeDtypeStruct((width, units), jnp.bfloat16),
        ],
        compiler_params=pltpu.CompilerParams(vmem_limit_bytes=56 << 20),
        cost_estimate=pl.CostEstimate(
            flops=6 * count * units * width, transcendentals=0, bytes_accessed=8 << 20
        ),
        name="feed_forward_grads",
    )(normed, cot, hidden, d_gate, d_up)


def split_features(values, parts):
    width = values.shape[1] // parts
    return jnp.stack([values[:, i * width : (i + 1) * width] for i in range(parts)])


def join_features(blocks):
    return jnp.concatenate([blocks[i] for i in range(blocks.shape[0])], axis=1)


def adam_update(master, mean_old, square_old, gradient, rate, decay):
    momentum = BETA_ONE * mean_old + (1.0 - BETA_ONE) * gradient
    variance = BETA_TWO * square_old + (1.0 - BETA_TWO) * gradient * gradient
    fix_one = 1.0 - BETA_ONE**ADAM_STEP
    fix_two = 1.0 - BETA_TWO**ADAM_STEP
    update = momentum / fix_one / (jnp.sqrt(variance / fix_two) + ADAM_EPS) + decay * master
    return (master - rate * update, momentum, variance)


def per_device(
    tokens,
    cotangent,
    prenorm_master,
    query_master,
    key_master_copy,
    value_master_copy,
    out_master,
    midnorm_master,
    gate_master,
    up_master,
    down_master,
    prenorm_mean,
    query_mean,
    key_first_moment,
    value_first_moment,
    out_mean,
    midnorm_mean,
    gate_mean,
    up_mean,
    down_mean,
    prenorm_square,
    query_square,
    key_second_moment,
    value_second_moment,
    out_square,
    midnorm_square,
    gate_square,
    up_square,
    down_square,
):
    masters = (
        prenorm_master,
        query_master,
        key_master_copy,
        value_master_copy,
        out_master,
        midnorm_master,
        gate_master,
        up_master,
        down_master,
    )
    low = jnp.bfloat16
    n_group, n_dp = lax.axis_size("group"), lax.axis_size("dp")
    my_group, my_dp = lax.axis_index("group"), lax.axis_index("dp")
    group_bits = [1 << i for i in range(n_group.bit_length() - 1)][::-1]
    dp_bits = [1 << i for i in range(n_dp.bit_length() - 1)][::-1]
    sizes = {"dp": n_dp, "group": n_group}
    places = {"dp": my_dp, "group": my_group}
    dp_steps = [("dp", bit) for bit in dp_bits]
    group_steps = [("group", bit) for bit in group_bits]
    far_steps, near_steps = group_steps[:-1], group_steps[-1:]
    wide_first = dp_steps + far_steps + near_steps
    far_first = far_steps + dp_steps + near_steps
    dp_twos, group_twos = (2,) * len(dp_bits), (2,) * len(group_bits)

    def gather_dp(block):
        held = gather_steps(block, dp_steps, sizes, places)
        return held.reshape((n_dp,) + block.shape)

    def gather_group(block):
        held = gather_steps(block, group_steps, sizes, places)
        return held.reshape((n_group,) + block.shape)

    def gather_tokens(block):
        held = block
        for axis, bit in group_steps:
            held = jnp.concatenate([held, swap(held, axis, bit, sizes[axis])], axis=0)
        return held

    def gather_both(block, steps):
        held = gather_steps(block, steps, sizes, places)
        return held.reshape((n_dp, n_group) + block.shape)

    def chain_both(blocks, steps):
        held = blocks.reshape(dp_twos + group_twos + blocks.shape[2:])
        return Chain(held, steps[::-1], dp_steps + group_steps, sizes, places)

    def chain_units(grads, steps):
        held = grads.reshape(dp_twos + (grads.shape[0] // n_dp, grads.shape[1]))
        return Chain(held, steps, dp_steps, sizes, places)

    def chain_tokens(values):
        return TokenChain(values, group_steps[::-1], (), sizes, places)

    rows = tokens.shape[0]
    width = tokens.shape[1]
    part = width // n_group
    gains = jnp.stack([prenorm_master, midnorm_master]).astype(low)
    gains_all = join_features(gather_group(gains)).astype(jnp.float32)
    gain_first, gain_second = gains_all[0:1], gains_all[1:2]

    query_block = query_master.astype(low).T
    kv_block = jnp.concatenate([key_master_copy.astype(low).T, value_master_copy.astype(low).T], axis=0)
    k_cols = key_master_copy.shape[1]
    w_query_t = gather_both(query_block, wide_first).swapaxes(0, 1).reshape(n_group, width, part)
    kv_blocks = gather_both(kv_block, far_first).swapaxes(0, 1)
    w_kv_t = jnp.concatenate(
        [
            kv_blocks[:, :, :k_cols].reshape(n_group, n_dp * k_cols, part),
            kv_blocks[:, :, k_cols:].reshape(n_group, n_dp * k_cols, part),
        ],
        axis=1,
    )
    w_out_t = gather_both(out_master.astype(low).T, wide_first).swapaxes(0, 1)
    w_out_t = w_out_t.reshape(n_group, width, part)

    unit = gate_master.shape[1] // n_group
    unit_rows = n_dp // n_group
    down_cols = down_master.shape[1]
    gate_up_block = jnp.concatenate(
        [
            gate_master.astype(low).T.reshape(n_group, unit, part),
            up_master.astype(low).T.reshape(n_group, unit, part),
        ],
        axis=1,
    )
    down_block = down_master.astype(low).reshape(unit_rows, n_group, unit, down_cols)
    down_block = down_block.transpose(1, 0, 2, 3).reshape(n_group, unit_rows * unit, down_cols)
    down_block = down_block.reshape(n_group, 2 * unit, part // 2)
    moved = jnp.concatenate([gate_up_block, down_block], axis=2)
    moved = lax.all_to_all(moved, "group", 0, 0, tiled=True)
    gate_up_block = join_features(moved[:, :, :part])
    down_block = moved[:, :, part:].reshape(n_dp * unit, down_cols).T
    w_gate_t = gather_dp(gate_up_block[:unit]).reshape(n_dp * unit, width)
    w_up_t = gather_dp(gate_up_block[unit:]).reshape(n_dp * unit, width)
    w_down_t = gather_dp(down_block).reshape(width, n_dp * unit)

    cot_held = gather_tokens(cotangent)

    sequence_count = rows // SEQUENCE_LENGTH
    heads_per_group = QUERY_HEADS // KEY_VALUE_HEADS
    score_scale = HEAD_SIZE ** (-0.5)
    q_width = QUERY_HEADS * HEAD_SIZE
    k_width = KEY_VALUE_HEADS * HEAD_SIZE
    tok_float = tokens.astype(jnp.float32)
    inv_one = lax.rsqrt(jnp.mean(tok_float * tok_float, axis=-1, keepdims=True) + EPS_NORM)
    scaled_one = tok_float * inv_one
    normed_one = (scaled_one * gain_first).astype(low)
    normed_rel = split_features(normed_one, n_group)

    def project(blocks, weights):
        total = dot(blocks[0], weights[0], 1, 1)
        for r in range(1, n_group):
            total = total + dot(blocks[r], weights[r], 1, 1)
        return total

    query_raw = project(normed_rel, w_query_t)
    kv_raw = project(normed_rel, w_kv_t)
    key_unrotated, value_projected = kv_raw[:, :k_width], kv_raw[:, k_width:]
    cosine_table, sine_table = rotary_tables(SEQUENCE_LENGTH, HEAD_SIZE)
    query_rotated = apply_rotation(
        query_raw.reshape(sequence_count, SEQUENCE_LENGTH, QUERY_HEADS, HEAD_SIZE),
        cosine_table,
        sine_table,
    ).astype(low)
    query_grouped = query_rotated.reshape(
        sequence_count, SEQUENCE_LENGTH, KEY_VALUE_HEADS, heads_per_group, HEAD_SIZE
    )
    key_rotated = apply_rotation(
        key_unrotated.reshape(sequence_count, SEQUENCE_LENGTH, KEY_VALUE_HEADS, HEAD_SIZE),
        cosine_table,
        sine_table,
    ).astype(low)
    value_reduced = value_projected.reshape(
        sequence_count, SEQUENCE_LENGTH, KEY_VALUE_HEADS, HEAD_SIZE
    ).astype(low)
    scores = weighted_values("sqkgd,spkd->skgqp", query_grouped, key_rotated) * score_scale
    causal = jnp.arange(SEQUENCE_LENGTH)[:, None] >= jnp.arange(SEQUENCE_LENGTH)[None, :]
    raw_weights = jnp.where(causal, jnp.exp(scores), 0.0)
    prob_full = raw_weights / jnp.sum(raw_weights, axis=-1, keepdims=True)
    probability_reduced = prob_full.astype(low)
    attended = weighted_values("skgqp,spkd->sqkgd", probability_reduced, value_reduced)
    attended_low = attended.reshape(rows, q_width).astype(low)
    attended_rel = split_features(attended_low, n_group)
    middle = tok_float + project(attended_rel, w_out_t)
    inv_two = lax.rsqrt(jnp.mean(middle * middle, axis=-1, keepdims=True) + EPS_NORM)
    scaled_two = middle * inv_two
    normed_two = (scaled_two * gain_second).astype(low)
    normed_all = gather_tokens(normed_two)
    d_normed_part, hidden, d_gate, d_up = feed_forward(
        normed_all, cot_held, w_gate_t, w_up_t, w_down_t
    )
    mid = chain_tokens(d_normed_part)
    got = mid.start()
    hidden, d_gate, d_up, got = lax.optimization_barrier((hidden, d_gate, d_up, got))
    mid.finish(got)
    got = mid.start()
    gate_grad, up_grad, down_grad = feed_forward_grads(normed_all, cot_held, hidden, d_gate, d_up)
    ffn = [
        chain_units(gate_grad, dp_steps[::-1]),
        chain_units(up_grad, dp_steps[::-1]),
        chain_units(down_grad, dp_steps[-2:-1] + dp_steps[:-2] + dp_steps[-1:]),
    ]
    mid.finish(got)
    d_normed_two = mid.total

    cot_float = cotangent.astype(jnp.float32)
    midnorm_sum = jnp.sum(d_normed_two * scaled_two, axis=0, keepdims=True)
    d_scaled_two = d_normed_two * gain_second
    d_middle = cot_float + inv_two * (
        d_scaled_two - scaled_two * jnp.mean(d_scaled_two * scaled_two, axis=-1, keepdims=True)
    )
    d_middle_low = d_middle.astype(low)

    def weight_grad(columns, blocks):
        return jnp.stack([dot(columns, blocks[r], 0, 0).astype(low) for r in range(n_group)])

    def input_part(columns, weights):
        return jnp.stack([dot(columns, weights[r], 1, 0) for r in range(n_group)])

    def by_owner(grads, columns):
        return grads.reshape(n_group, n_dp, columns, part).swapaxes(0, 1)

    out_chain = chain_both(
        by_owner(weight_grad(d_middle_low, attended_rel), width // n_dp), wide_first
    )
    finish_all([out_chain], start_all([out_chain]))
    attended_gradient = join_features(input_part(d_middle_low, w_out_t).astype(low))
    attended_gradient = attended_gradient.reshape(
        sequence_count, SEQUENCE_LENGTH, KEY_VALUE_HEADS, heads_per_group, HEAD_SIZE
    )
    d_prob = weighted_values("sqkgd,spkd->skgqp", attended_gradient, value_reduced)
    inner_sum = jnp.sum(prob_full * d_prob, axis=-1, keepdims=True)
    d_score = (prob_full * (d_prob - inner_sum) * score_scale).astype(low)
    d_query = weighted_values("skgqp,spkd->sqkgd", d_score, key_rotated).reshape(
        sequence_count, SEQUENCE_LENGTH, QUERY_HEADS, HEAD_SIZE
    )
    d_query = inverse_rotation(d_query, cosine_table, sine_table).reshape(rows, q_width).astype(low)
    key_gradient = weighted_values("fceti,ftcel->ficl", d_score, query_grouped)
    key_gradient = (
        inverse_rotation(key_gradient, cosine_table, sine_table).reshape(rows, k_width).astype(low)
    )
    value_gradient = (
        weighted_values("fceti,ftcel->ficl", probability_reduced, attended_gradient)
        .reshape(rows, k_width)
        .astype(low)
    )
    kv_gradient = jnp.concatenate([key_gradient, value_gradient], axis=1)
    d_normed_blocks = input_part(d_query, w_query_t) + input_part(kv_gradient, w_kv_t)
    d_normed_one = join_features(d_normed_blocks)
    prenorm_sum = jnp.sum(d_normed_one * scaled_one, axis=0, keepdims=True)
    d_scaled_one = d_normed_one * gain_first
    input_grad = d_middle + inv_one * (
        d_scaled_one - scaled_one * jnp.mean(d_scaled_one * scaled_one, axis=-1, keepdims=True)
    )
    gain_rows = jnp.concatenate([prenorm_sum, midnorm_sum], axis=0)

    query_chain = chain_both(by_owner(weight_grad(d_query, normed_rel), q_width // n_dp), wide_first)
    kv_sum = jnp.concatenate(
        [
            by_owner(weight_grad(key_gradient, normed_rel), k_cols),
            by_owner(weight_grad(value_gradient, normed_rel), k_cols),
        ],
        axis=2,
    )
    kv_chain = chain_both(kv_sum, far_first)
    gain_held = split_features(gain_rows, n_group).astype(low).reshape(group_twos + (2, part))
    gain_chain = Chain(gain_held, group_steps[::-1] + dp_steps, group_steps, sizes, places)
    hidden_late, _ = lax.optimization_barrier((hidden, d_score))
    out_part = dot(hidden_late, w_down_t, 1, 1)
    token_chain = chain_tokens(out_part.astype(low))
    pace = [query_chain, kv_chain, out_chain, gain_chain, token_chain]
    pending = start_all(ffn)
    count = 0
    while any(chain.steps for chain in pace):
        live = [chain for chain in pace if chain.steps]
        gots = finish_all(live, start_all(live))
        if count != 2 or not any(chain.steps for chain in pace):
            while pending:
                finish_all(ffn, pending, gots[:1])
                pending = start_all(ffn) if ffn[0].steps else ()
                if any(chain.steps for chain in pace):
                    break
        count += 1
    query_own, out_own = query_chain.total.T, out_chain.total.T
    kv_own = kv_chain.total
    key_own, value_own = kv_own[:k_cols].T, kv_own[k_cols:].T
    prenorm_own, midnorm_own = gain_chain.total[0], gain_chain.total[1]
    output = middle + token_chain.total

    gate_up_back = split_features(jnp.concatenate([ffn[0].held, ffn[1].held], axis=0), n_group)
    down_back = ffn[2].held.T.reshape(n_group, unit_rows * unit, down_cols)
    down_back = down_back.reshape(n_group, 2 * unit, part // 2)
    back = jnp.concatenate([gate_up_back, down_back], axis=2)
    back = lax.all_to_all(back, "group", 0, 0, tiled=True)
    gate_own = back[:, :unit, :part].reshape(n_group * unit, part).T.astype(jnp.float32)
    up_own = back[:, unit:, :part].reshape(n_group * unit, part).T.astype(jnp.float32)
    down_back = back[:, :, part:].reshape(n_group, unit_rows, unit, down_cols).transpose(1, 0, 2, 3)
    down_own = down_back.reshape(n_dp * unit, down_cols).astype(jnp.float32)
    owned = (
        prenorm_own,
        query_own,
        key_own,
        value_own,
        out_own,
        midnorm_own,
        gate_own,
        up_own,
        down_own,
    )
    mean_list = (
        prenorm_mean,
        query_mean,
        key_first_moment,
        value_first_moment,
        out_mean,
        midnorm_mean,
        gate_mean,
        up_mean,
        down_mean,
    )
    square_list = (
        prenorm_square,
        query_square,
        key_second_moment,
        value_second_moment,
        out_square,
        midnorm_square,
        gate_square,
        up_square,
        down_square,
    )
    rate_list = (
        RATE_GAIN,
        RATE_MATRIX,
        RATE_MATRIX,
        RATE_MATRIX,
        RATE_OUTPUT,
        RATE_GAIN,
        RATE_MATRIX,
        RATE_MATRIX,
        RATE_MATRIX,
    )
    decays = (
        0.0,
        DECAY_RATE,
        DECAY_RATE,
        DECAY_RATE,
        DECAY_RATE,
        0.0,
        DECAY_RATE,
        DECAY_RATE,
        DECAY_RATE,
    )
    results = [
        adam_update(masters[k], mean_list[k], square_list[k], owned[k], rate_list[k], decays[k])
        for k in range(9)
    ]
    return (
        output,
        input_grad,
        owned[0],
        owned[1],
        owned[2],
        owned[3],
        owned[4],
        owned[5],
        owned[6],
        owned[7],
        owned[8],
        results[0][0],
        results[1][0],
        results[2][0],
        results[3][0],
        results[4][0],
        results[5][0],
        results[6][0],
        results[7][0],
        results[8][0],
        results[0][1],
        results[1][1],
        results[2][1],
        results[3][1],
        results[4][1],
        results[5][1],
        results[6][1],
        results[7][1],
        results[8][1],
        results[0][2],
        results[1][2],
        results[2][2],
        results[3][2],
        results[4][2],
        results[5][2],
        results[6][2],
        results[7][2],
        results[8][2],
    )


def solution(mesh):
    placed = (
        P(("dp", "group"), None),
        P(("dp", "group"), None),
        P("group"),
        P("group", "dp"),
        P("group", "dp"),
        P("group", "dp"),
        P("group", "dp"),
        P("group"),
        P("group", "dp"),
        P("group", "dp"),
        P("group", "dp"),
        P("group"),
        P("group", "dp"),
        P("group", "dp"),
        P("group", "dp"),
        P("group", "dp"),
        P("group"),
        P("group", "dp"),
        P("group", "dp"),
        P("group", "dp"),
        P("group"),
        P("group", "dp"),
        P("group", "dp"),
        P("group", "dp"),
        P("group", "dp"),
        P("group"),
        P("group", "dp"),
        P("group", "dp"),
        P("group", "dp"),
    )
    return jax.shard_map(
        per_device,
        mesh=mesh,
        in_specs=placed,
        out_specs=(
            P(("dp", "group"), None),
            P(("dp", "group"), None),
            P("group"),
            P("group", "dp"),
            P("group", "dp"),
            P("group", "dp"),
            P("group", "dp"),
            P("group"),
            P("group", "dp"),
            P("group", "dp"),
            P("group", "dp"),
            P("group"),
            P("group", "dp"),
            P("group", "dp"),
            P("group", "dp"),
            P("group", "dp"),
            P("group"),
            P("group", "dp"),
            P("group", "dp"),
            P("group", "dp"),
            P("group"),
            P("group", "dp"),
            P("group", "dp"),
            P("group", "dp"),
            P("group", "dp"),
            P("group"),
            P("group", "dp"),
            P("group", "dp"),
            P("group", "dp"),
            P("group"),
            P("group", "dp"),
            P("group", "dp"),
            P("group", "dp"),
            P("group", "dp"),
            P("group"),
            P("group", "dp"),
            P("group", "dp"),
            P("group", "dp"),
        ),
        check_vma=False,
    )
```

```python
import jax
import jax.numpy as jnp
from jax import lax
from jax.experimental import pallas as pl
from jax.experimental.layout import Layout, with_layout_constraint
from jax.experimental.pallas import tpu as pltpu
from jax.sharding import PartitionSpec as P

QUERY_HEADS = 15
KEY_VALUE_HEADS = 5
HEAD_SIZE = 64
SEQUENCE_LENGTH = 128


EPS_NORM = 1e-05
BETA_ONE = 0.9
BETA_TWO = 0.95
ADAM_EPS = 1e-08
RATE_MATRIX = 0.015
RATE_OUTPUT = 0.05
RATE_GAIN = 0.4
DECAY_RATE = 0.1
ADAM_STEP = 4.0
ROPE_BASE = 10000.0


def weighted_values(pattern, left_op, right_op):
    return jnp.einsum(pattern, left_op, right_op, preferred_element_type=jnp.float32)


def rotary_tables(length, head_dim):
    half_dim = head_dim // 2
    frequency = ROPE_BASE ** (-(jnp.arange(half_dim, dtype=jnp.float32) * 2.0 / head_dim))
    angles = jnp.arange(length, dtype=jnp.float32)[:, None] * frequency[None, :]
    return (jnp.cos(angles), jnp.sin(angles))


def apply_rotation(values, cosine_table, sine_table):
    half_dim = values.shape[-1] // 2
    first_half = values[..., :half_dim]
    second = values[..., half_dim:]
    cos_part = cosine_table[:, None, :]
    sin_part = sine_table[:, None, :]
    return jnp.concatenate(
        [first_half * cos_part - second * sin_part, second * cos_part + first_half * sin_part],
        axis=-1,
    )


def inverse_rotation(values, cosine_table, sine_table):
    half_dim = values.shape[-1] // 2
    first_half = values[..., :half_dim]
    second = values[..., half_dim:]
    cos_part = cosine_table[:, None, :]
    sin_part = sine_table[:, None, :]
    return jnp.concatenate(
        [first_half * cos_part + second * sin_part, second * cos_part - first_half * sin_part],
        axis=-1,
    )


def swap(value, axis, bit, size):
    return lax.ppermute(value, axis, [(i, i ^ bit) for i in range(size)])


def gather_steps(value, steps, sizes, places):
    held, done = value, []
    for axis, bit in steps:
        got = swap(held, axis, bit, sizes[axis])
        upper = (places[axis] & bit) != 0
        at = len([d for d in done if (d[0] == "dp" and axis == "group") or (d[0] == axis and d[1] > bit)])
        low_part, high_part = jnp.where(upper, got, held), jnp.where(upper, held, got)
        held = jnp.stack([low_part, high_part], axis=at)
        done = done + [(axis, bit)]
    return held


class Chain:
    def __init__(self, held, steps, done, sizes, places):
        self.held, self.steps, self.done = held, list(steps), list(done)
        self.sizes, self.places = sizes, places

    def start(self):
        axis, bit = self.steps.pop(0)
        if (axis, bit) in self.done:
            at = self.done.index((axis, bit))
            mine = ((self.places[axis] & bit) != 0).astype(jnp.int32)
            sent = lax.dynamic_index_in_dim(self.held, 1 - mine, at, keepdims=False)
            self.kept = lax.dynamic_index_in_dim(self.held, mine, at, keepdims=False)
            self.done.pop(at)
        else:
            sent = self.kept = self.held
        return swap(sent, axis, bit, self.sizes[axis])

    def finish(self, got):
        self.total = self.kept.astype(jnp.float32) + got.astype(jnp.float32)
        self.held = self.total.astype(jnp.bfloat16)


class TokenChain(Chain):
    def start(self):
        axis, bit = self.steps.pop(0)
        half = self.held.shape[0] // 2
        self.kept = self.held[:half]
        return swap(self.held[half:], axis, bit, self.sizes[axis])


def start_all(chains):
    return tuple(chain.start() for chain in chains)


def finish_all(chains, gots, behind=()):
    gots = lax.optimization_barrier(tuple(gots) + tuple(behind))[: len(gots)]
    for chain, got in zip(chains, gots):
        chain.finish(got)
    return gots


def dot(left_op, right_op, left_dim, right_dim):
    return lax.dot_general(
        left_op, right_op, (((left_dim,), (right_dim,)), ((), ())), preferred_element_type=jnp.float32
    )


def mix_kernel(normed_ref, cot_ref, gate_ref, up_ref, down_ref, kept_ref, sent_ref, hidden_ref, dg_ref, du_ref):
    normed = normed_ref[...]
    gate_value = dot(normed, gate_ref[...], 1, 1)
    up_value = dot(normed, up_ref[...], 1, 1)
    d_hidden = dot(cot_ref[...], down_ref[...], 1, 0)
    sigmoid_gate = jax.nn.sigmoid(gate_value)
    silu_gate = gate_value * sigmoid_gate
    hidden_ref[...] = (silu_gate * up_value).astype(jnp.bfloat16)
    d_gate = (
        d_hidden * up_value * sigmoid_gate * (1.0 + gate_value * (1.0 - sigmoid_gate))
    ).astype(jnp.bfloat16)
    d_up = (d_hidden * silu_gate).astype(jnp.bfloat16)
    dg_ref[...] = d_gate
    du_ref[...] = d_up
    d_normed = dot(d_gate, gate_ref[...], 1, 0) + dot(d_up, up_ref[...], 1, 0)

    @pl.when(pl.program_id(0) == 0)
    def _():
        kept_ref[...] = d_normed.astype(jnp.bfloat16)

    @pl.when(pl.program_id(0) == 1)
    def _():
        sent_ref[...] = d_normed.astype(jnp.bfloat16)


def feed_forward(normed, cot, w_gate_t, w_up_t, w_down_t):
    count, width = normed.shape
    units = w_gate_t.shape[0]
    step = count // 2
    whole = lambda shape: pl.BlockSpec(shape, lambda i: (0, 0))
    rows = lambda cols: pl.BlockSpec((step, cols), lambda i: (i, 0))
    shape = lambda cols: jax.ShapeDtypeStruct((count, cols), jnp.bfloat16)
    return pl.pallas_call(
        mix_kernel,
        grid=(2,),
        in_specs=[
            rows(width),
            rows(width),
            whole((units, width)),
            whole((units, width)),
            whole((width, units)),
        ],
        out_specs=[whole((step, width)), whole((step, width)), rows(units), rows(units), rows(units)],
        out_shape=[jax.ShapeDtypeStruct((step, width), jnp.bfloat16)] * 2
        + [shape(units), shape(units), shape(units)],
        compiler_params=pltpu.CompilerParams(vmem_limit_bytes=56 << 20),
        cost_estimate=pl.CostEstimate(
            flops=10 * count * units * width, transcendentals=count * units, bytes_accessed=12 << 20
        ),
        name="feed_forward",
    )(normed, cot, w_gate_t, w_up_t, w_down_t)


def grad_kernel(normed_ref, cot_ref, hidden_ref, dg_ref, du_ref, pair_ref, down_ref):
    pair_ref[0] = dot(dg_ref[...], normed_ref[...], 0, 0).astype(jnp.bfloat16)
    pair_ref[1] = dot(du_ref[...], normed_ref[...], 0, 0).astype(jnp.bfloat16)
    down_ref[...] = dot(cot_ref[...], hidden_ref[...], 0, 0).astype(jnp.bfloat16)


def feed_forward_grads(normed, cot, hidden, d_gate, d_up):
    count, width = normed.shape
    units = hidden.shape[1]
    vmem = pl.BlockSpec(memory_space=pltpu.VMEM)
    return pl.pallas_call(
        grad_kernel,
        in_specs=[vmem] * 5,
        out_specs=[vmem] * 2,
        out_shape=[
            jax.ShapeDtypeStruct((2, units, width), jnp.bfloat16),
            jax.ShapeDtypeStruct((width, units), jnp.bfloat16),
        ],
        compiler_params=pltpu.CompilerParams(vmem_limit_bytes=56 << 20),
        cost_estimate=pl.CostEstimate(
            flops=6 * count * units * width, transcendentals=0, bytes_accessed=8 << 20
        ),
        name="feed_forward_grads",
    )(normed, cot, hidden, d_gate, d_up)


def row_major(value):
    return with_layout_constraint(value, Layout(major_to_minor=tuple(range(value.ndim))))


def split_features(values, parts):
    width = values.shape[1] // parts
    return jnp.stack([values[:, i * width : (i + 1) * width] for i in range(parts)])


def join_features(blocks):
    return jnp.concatenate([blocks[i] for i in range(blocks.shape[0])], axis=1)


def adam_update(master, mean_old, square_old, gradient, rate, decay):
    momentum = BETA_ONE * mean_old + (1.0 - BETA_ONE) * gradient
    variance = BETA_TWO * square_old + (1.0 - BETA_TWO) * gradient * gradient
    fix_one = 1.0 - BETA_ONE**ADAM_STEP
    fix_two = 1.0 - BETA_TWO**ADAM_STEP
    update = momentum / fix_one / (jnp.sqrt(variance / fix_two) + ADAM_EPS) + decay * master
    return (master - rate * update, momentum, variance)


def per_device(
    tokens,
    cotangent,
    prenorm_master,
    query_master,
    key_master_copy,
    value_master_copy,
    out_master,
    midnorm_master,
    gate_master,
    up_master,
    down_master,
    prenorm_mean,
    query_mean,
    key_first_moment,
    value_first_moment,
    out_mean,
    midnorm_mean,
    gate_mean,
    up_mean,
    down_mean,
    prenorm_square,
    query_square,
    key_second_moment,
    value_second_moment,
    out_square,
    midnorm_square,
    gate_square,
    up_square,
    down_square,
):
    masters = (
        prenorm_master,
        query_master,
        key_master_copy,
        value_master_copy,
        out_master,
        midnorm_master,
        gate_master,
        up_master,
        down_master,
    )
    low = jnp.bfloat16
    n_group, n_dp = lax.axis_size("group"), lax.axis_size("dp")
    my_group, my_dp = lax.axis_index("group"), lax.axis_index("dp")
    group_bits = [1 << i for i in range(n_group.bit_length() - 1)][::-1]
    dp_bits = [1 << i for i in range(n_dp.bit_length() - 1)][::-1]
    sizes = {"dp": n_dp, "group": n_group}
    places = {"dp": my_dp, "group": my_group}
    dp_steps = [("dp", bit) for bit in dp_bits]
    group_steps = [("group", bit) for bit in group_bits]
    far_steps, near_steps = group_steps[:-1], group_steps[-1:]
    wide_first = dp_steps + far_steps + near_steps
    far_first = far_steps + dp_steps + near_steps
    dp_twos, group_twos = (2,) * len(dp_bits), (2,) * len(group_bits)

    def gather_dp(block):
        held = gather_steps(block, dp_steps, sizes, places)
        return held.reshape((n_dp,) + block.shape)

    def gather_group(block):
        held = gather_steps(block, group_steps, sizes, places)
        return held.reshape((n_group,) + block.shape)

    def gather_tokens(block):
        held = block
        for axis, bit in group_steps:
            held = jnp.concatenate([held, swap(held, axis, bit, sizes[axis])], axis=0)
        return held

    def gather_both(block, steps):
        held = gather_steps(block, steps, sizes, places)
        return held.reshape((n_dp, n_group) + block.shape)

    def chain_both(blocks, steps):
        held = blocks.reshape(dp_twos + group_twos + blocks.shape[2:])
        return Chain(held, steps[::-1], dp_steps + group_steps, sizes, places)

    def chain_units(grads, steps):
        held = grads.reshape(dp_twos + (grads.shape[0] // n_dp, grads.shape[1]))
        return Chain(held, steps, dp_steps, sizes, places)

    def chain_tokens(values):
        return TokenChain(values, group_steps[::-1], (), sizes, places)

    rows = tokens.shape[0]
    width = tokens.shape[1]
    part = width // n_group
    gains = jnp.stack([prenorm_master, midnorm_master]).astype(low)
    gains_all = join_features(gather_group(gains)).astype(jnp.float32)
    gain_first, gain_second = gains_all[0:1], gains_all[1:2]

    query_block = query_master.astype(low).T
    kv_block = jnp.concatenate([key_master_copy.astype(low).T, value_master_copy.astype(low).T], axis=0)
    k_cols = key_master_copy.shape[1]
    w_query_t = gather_both(query_block, wide_first).swapaxes(0, 1).reshape(n_group, width, part)
    kv_blocks = gather_both(kv_block, far_first).swapaxes(0, 1)
    w_kv_t = jnp.concatenate(
        [
            kv_blocks[:, :, :k_cols].reshape(n_group, n_dp * k_cols, part),
            kv_blocks[:, :, k_cols:].reshape(n_group, n_dp * k_cols, part),
        ],
        axis=1,
    )
    w_out_t = gather_both(out_master.astype(low).T, wide_first).swapaxes(0, 1)
    w_out_t = w_out_t.reshape(n_group, width, part)

    unit = gate_master.shape[1] // n_group
    unit_rows = n_dp // n_group
    down_cols = down_master.shape[1]
    gate_up_block = jnp.concatenate(
        [
            gate_master.astype(low).T.reshape(n_group, unit, part),
            up_master.astype(low).T.reshape(n_group, unit, part),
        ],
        axis=1,
    )
    down_block = down_master.astype(low).reshape(unit_rows, n_group, unit, down_cols)
    down_block = down_block.transpose(1, 0, 2, 3).reshape(n_group, unit_rows * unit, down_cols)
    down_block = down_block.reshape(n_group, 2 * unit, part // 2)
    moved = jnp.concatenate([gate_up_block, down_block], axis=2)
    moved = lax.all_to_all(moved, "group", 0, 0, tiled=True)
    gate_up_block = join_features(moved[:, :, :part])
    down_block = row_major(moved[:, :, part:].reshape(n_dp * unit, down_cols).T)
    w_gate_t = gather_dp(gate_up_block[:unit]).reshape(n_dp * unit, width)
    w_up_t = gather_dp(gate_up_block[unit:]).reshape(n_dp * unit, width)
    w_down_t = gather_dp(down_block).reshape(width, n_dp * unit)

    cot_held = gather_tokens(cotangent)

    sequence_count = rows // SEQUENCE_LENGTH
    heads_per_group = QUERY_HEADS // KEY_VALUE_HEADS
    score_scale = HEAD_SIZE ** (-0.5)
    q_width = QUERY_HEADS * HEAD_SIZE
    k_width = KEY_VALUE_HEADS * HEAD_SIZE
    tok_float = tokens.astype(jnp.float32)
    inv_one = lax.rsqrt(jnp.mean(tok_float * tok_float, axis=-1, keepdims=True) + EPS_NORM)
    scaled_one = tok_float * inv_one
    normed_one = (scaled_one * gain_first).astype(low)
    normed_rel = split_features(normed_one, n_group)

    def project(blocks, weights):
        total = dot(blocks[0], weights[0], 1, 1)
        for r in range(1, n_group):
            total = total + dot(blocks[r], weights[r], 1, 1)
        return total

    query_raw = project(normed_rel, w_query_t)
    kv_raw = project(normed_rel, w_kv_t)
    key_unrotated, value_projected = kv_raw[:, :k_width], kv_raw[:, k_width:]
    cosine_table, sine_table = rotary_tables(SEQUENCE_LENGTH, HEAD_SIZE)
    query_rotated = apply_rotation(
        query_raw.reshape(sequence_count, SEQUENCE_LENGTH, QUERY_HEADS, HEAD_SIZE),
        cosine_table,
        sine_table,
    ).astype(low)
    query_grouped = query_rotated.reshape(
        sequence_count, SEQUENCE_LENGTH, KEY_VALUE_HEADS, heads_per_group, HEAD_SIZE
    )
    key_rotated = apply_rotation(
        key_unrotated.reshape(sequence_count, SEQUENCE_LENGTH, KEY_VALUE_HEADS, HEAD_SIZE),
        cosine_table,
        sine_table,
    ).astype(low)
    value_reduced = value_projected.reshape(
        sequence_count, SEQUENCE_LENGTH, KEY_VALUE_HEADS, HEAD_SIZE
    ).astype(low)
    scores = weighted_values("sqkgd,spkd->skgqp", query_grouped, key_rotated) * score_scale
    causal = jnp.arange(SEQUENCE_LENGTH)[:, None] >= jnp.arange(SEQUENCE_LENGTH)[None, :]
    raw_weights = jnp.where(causal, jnp.exp(scores), 0.0)
    prob_full = raw_weights / jnp.sum(raw_weights, axis=-1, keepdims=True)
    probability_reduced = prob_full.astype(low)
    attended = weighted_values("skgqp,spkd->sqkgd", probability_reduced, value_reduced)
    attended_low = attended.reshape(rows, q_width).astype(low)
    attended_rel = split_features(attended_low, n_group)
    middle = tok_float + project(attended_rel, w_out_t)
    inv_two = lax.rsqrt(jnp.mean(middle * middle, axis=-1, keepdims=True) + EPS_NORM)
    scaled_two = middle * inv_two
    normed_two = (scaled_two * gain_second).astype(low)
    normed_all = gather_tokens(normed_two)
    d_normed_kept, d_normed_sent, hidden, d_gate, d_up = feed_forward(
        normed_all, cot_held, w_gate_t, w_up_t, w_down_t
    )
    mid = TokenChain(None, group_steps[::-1], (), sizes, places)
    axis, bit = mid.steps.pop(0)
    mid.kept = d_normed_kept
    got = swap(d_normed_sent, axis, bit, sizes[axis])
    hidden, d_gate, d_up, got = lax.optimization_barrier((hidden, d_gate, d_up, got))
    mid.finish(got)
    got = mid.start()
    pair_grad, down_grad = feed_forward_grads(normed_all, cot_held, hidden, d_gate, d_up)
    ffn = [
        Chain(
            pair_grad.reshape((2,) + dp_twos + (unit, width)),
            dp_steps[::-1],
            [("pair", 0)] + dp_steps,
            sizes,
            places,
        ),
        chain_units(down_grad, dp_steps[-2:-1] + dp_steps[:-2] + dp_steps[-1:]),
    ]
    mid.finish(got)
    d_normed_two = mid.total

    cot_float = cotangent.astype(jnp.float32)
    midnorm_sum = jnp.sum(d_normed_two * scaled_two, axis=0, keepdims=True)
    d_scaled_two = d_normed_two * gain_second
    d_middle = cot_float + inv_two * (
        d_scaled_two - scaled_two * jnp.mean(d_scaled_two * scaled_two, axis=-1, keepdims=True)
    )
    d_middle_low = d_middle.astype(low)

    def weight_grad(columns, blocks):
        return jnp.stack([dot(columns, blocks[r], 0, 0).astype(low) for r in range(n_group)])

    def input_part(columns, weights):
        return jnp.stack([dot(columns, weights[r], 1, 0) for r in range(n_group)])

    def by_owner(grads, columns):
        return grads.reshape(n_group, n_dp, columns, part).swapaxes(0, 1)

    out_chain = chain_both(
        by_owner(weight_grad(d_middle_low, attended_rel), width // n_dp), wide_first
    )
    finish_all([out_chain], start_all([out_chain]))
    attended_gradient = join_features(input_part(d_middle_low, w_out_t).astype(low))
    attended_gradient = attended_gradient.reshape(
        sequence_count, SEQUENCE_LENGTH, KEY_VALUE_HEADS, heads_per_group, HEAD_SIZE
    )
    d_prob = weighted_values("sqkgd,spkd->skgqp", attended_gradient, value_reduced)
    inner_sum = jnp.sum(prob_full * d_prob, axis=-1, keepdims=True)
    d_score = (prob_full * (d_prob - inner_sum) * score_scale).astype(low)
    d_query = weighted_values("skgqp,spkd->sqkgd", d_score, key_rotated).reshape(
        sequence_count, SEQUENCE_LENGTH, QUERY_HEADS, HEAD_SIZE
    )
    d_query = inverse_rotation(d_query, cosine_table, sine_table).reshape(rows, q_width).astype(low)
    key_gradient = weighted_values("fceti,ftcel->ficl", d_score, query_grouped)
    key_gradient = (
        inverse_rotation(key_gradient, cosine_table, sine_table).reshape(rows, k_width).astype(low)
    )
    value_gradient = (
        weighted_values("fceti,ftcel->ficl", probability_reduced, attended_gradient)
        .reshape(rows, k_width)
        .astype(low)
    )
    kv_gradient = jnp.concatenate([key_gradient, value_gradient], axis=1)
    d_normed_blocks = input_part(d_query, w_query_t) + input_part(kv_gradient, w_kv_t)
    d_normed_one = join_features(d_normed_blocks)
    prenorm_sum = jnp.sum(d_normed_one * scaled_one, axis=0, keepdims=True)
    d_scaled_one = d_normed_one * gain_first
    input_grad = d_middle + inv_one * (
        d_scaled_one - scaled_one * jnp.mean(d_scaled_one * scaled_one, axis=-1, keepdims=True)
    )
    gain_rows = jnp.concatenate([prenorm_sum, midnorm_sum], axis=0)

    query_chain = chain_both(by_owner(weight_grad(d_query, normed_rel), q_width // n_dp), wide_first)
    kv_sum = jnp.concatenate(
        [
            by_owner(weight_grad(key_gradient, normed_rel), k_cols),
            by_owner(weight_grad(value_gradient, normed_rel), k_cols),
        ],
        axis=2,
    )
    kv_chain = chain_both(kv_sum, far_first)
    gain_held = split_features(gain_rows, n_group).astype(low).reshape(group_twos + (2, part))
    gain_chain = Chain(gain_held, group_steps[::-1] + dp_steps, group_steps, sizes, places)
    hidden_late, _ = lax.optimization_barrier((hidden, d_score))
    out_part = dot(hidden_late, w_down_t, 1, 1)
    token_chain = chain_tokens(out_part.astype(low))
    pace = [query_chain, kv_chain, out_chain, gain_chain, token_chain]
    pending = start_all(ffn)
    count = 0
    while any(chain.steps for chain in pace):
        live = [chain for chain in pace if chain.steps]
        gots = finish_all(live, start_all(live))
        if count != 2 or not any(chain.steps for chain in pace):
            while pending:
                finish_all(ffn, pending, gots[:1])
                pending = start_all(ffn) if ffn[0].steps else ()
                if any(chain.steps for chain in pace):
                    break
        count += 1
    query_own = row_major(row_major(query_chain.total).T)
    out_own = row_major(row_major(out_chain.total).T)
    kv_own = kv_chain.total
    key_own, value_own = kv_own[:k_cols].T, kv_own[k_cols:].T
    prenorm_own, midnorm_own = gain_chain.total[0], gain_chain.total[1]
    output = middle + token_chain.total

    gate_up_back = split_features(ffn[0].held.reshape(2 * unit, width), n_group)
    down_back = row_major(ffn[1].held).T.reshape(n_group, unit_rows * unit, down_cols)
    down_back = down_back.reshape(n_group, 2 * unit, part // 2)
    back = jnp.concatenate([gate_up_back, down_back], axis=2)
    back = lax.all_to_all(back, "group", 0, 0, tiled=True)
    gate_own = back[:, :unit, :part].reshape(n_group * unit, part).T.astype(jnp.float32)
    up_own = back[:, unit:, :part].reshape(n_group * unit, part).T.astype(jnp.float32)
    down_back = back[:, :, part:].reshape(n_group, unit_rows, unit, down_cols).transpose(1, 0, 2, 3)
    down_own = down_back.reshape(n_dp * unit, down_cols).astype(jnp.float32)
    down_own = with_layout_constraint(down_own, Layout(major_to_minor=(1, 0)))
    owned = (
        prenorm_own,
        query_own,
        key_own,
        value_own,
        out_own,
        midnorm_own,
        gate_own,
        up_own,
        down_own,
    )
    mean_list = (
        prenorm_mean,
        query_mean,
        key_first_moment,
        value_first_moment,
        out_mean,
        midnorm_mean,
        gate_mean,
        up_mean,
        down_mean,
    )
    square_list = (
        prenorm_square,
        query_square,
        key_second_moment,
        value_second_moment,
        out_square,
        midnorm_square,
        gate_square,
        up_square,
        down_square,
    )
    rate_list = (
        RATE_GAIN,
        RATE_MATRIX,
        RATE_MATRIX,
        RATE_MATRIX,
        RATE_OUTPUT,
        RATE_GAIN,
        RATE_MATRIX,
        RATE_MATRIX,
        RATE_MATRIX,
    )
    decays = (
        0.0,
        DECAY_RATE,
        DECAY_RATE,
        DECAY_RATE,
        DECAY_RATE,
        0.0,
        DECAY_RATE,
        DECAY_RATE,
        DECAY_RATE,
    )
    results = [
        adam_update(masters[k], mean_list[k], square_list[k], owned[k], rate_list[k], decays[k])
        for k in range(9)
    ]
    return (
        output,
        input_grad,
        owned[0],
        owned[1],
        owned[2],
        owned[3],
        owned[4],
        owned[5],
        owned[6],
        owned[7],
        owned[8],
        results[0][0],
        results[1][0],
        results[2][0],
        results[3][0],
        results[4][0],
        results[5][0],
        results[6][0],
        results[7][0],
        results[8][0],
        results[0][1],
        results[1][1],
        results[2][1],
        results[3][1],
        results[4][1],
        results[5][1],
        results[6][1],
        results[7][1],
        results[8][1],
        results[0][2],
        results[1][2],
        results[2][2],
        results[3][2],
        results[4][2],
        results[5][2],
        results[6][2],
        results[7][2],
        results[8][2],
    )


def solution(mesh):
    placed = (
        P(("dp", "group"), None),
        P(("dp", "group"), None),
        P("group"),
        P("group", "dp"),
        P("group", "dp"),
        P("group", "dp"),
        P("group", "dp"),
        P("group"),
        P("group", "dp"),
        P("group", "dp"),
        P("group", "dp"),
        P("group"),
        P("group", "dp"),
        P("group", "dp"),
        P("group", "dp"),
        P("group", "dp"),
        P("group"),
        P("group", "dp"),
        P("group", "dp"),
        P("group", "dp"),
        P("group"),
        P("group", "dp"),
        P("group", "dp"),
        P("group", "dp"),
        P("group", "dp"),
        P("group"),
        P("group", "dp"),
        P("group", "dp"),
        P("group", "dp"),
    )
    return jax.shard_map(
        per_device,
        mesh=mesh,
        in_specs=placed,
        out_specs=(
            P(("dp", "group"), None),
            P(("dp", "group"), None),
            P("group"),
            P("group", "dp"),
            P("group", "dp"),
            P("group", "dp"),
            P("group", "dp"),
            P("group"),
            P("group", "dp"),
            P("group", "dp"),
            P("group", "dp"),
            P("group"),
            P("group", "dp"),
            P("group", "dp"),
            P("group", "dp"),
            P("group", "dp"),
            P("group"),
            P("group", "dp"),
            P("group", "dp"),
            P("group", "dp"),
            P("group"),
            P("group", "dp"),
            P("group", "dp"),
            P("group", "dp"),
            P("group", "dp"),
            P("group"),
            P("group", "dp"),
            P("group", "dp"),
            P("group", "dp"),
            P("group"),
            P("group", "dp"),
            P("group", "dp"),
            P("group", "dp"),
            P("group", "dp"),
            P("group"),
            P("group", "dp"),
            P("group", "dp"),
            P("group", "dp"),
        ),
        check_vma=False,
    )
```

```python
import jax
import jax.numpy as jnp
from jax import lax
from jax.experimental import pallas as pl
from jax.experimental.layout import Layout, with_layout_constraint
from jax.experimental.pallas import tpu as pltpu
from jax.sharding import PartitionSpec as P

QUERY_HEADS = 15
KEY_VALUE_HEADS = 5
HEAD_SIZE = 64
SEQUENCE_LENGTH = 128


EPS_NORM = 1e-05
BETA_ONE = 0.9
BETA_TWO = 0.95
ADAM_EPS = 1e-08
RATE_MATRIX = 0.015
RATE_OUTPUT = 0.05
RATE_GAIN = 0.4
DECAY_RATE = 0.1
ADAM_STEP = 4.0
ROPE_BASE = 10000.0


def weighted_values(pattern, left_op, right_op):
    return jnp.einsum(pattern, left_op, right_op, preferred_element_type=jnp.float32)


def rotary_tables(length, head_dim):
    half_dim = head_dim // 2
    frequency = ROPE_BASE ** (-(jnp.arange(half_dim, dtype=jnp.float32) * 2.0 / head_dim))
    angles = jnp.arange(length, dtype=jnp.float32)[:, None] * frequency[None, :]
    return (jnp.cos(angles), jnp.sin(angles))


def apply_rotation(values, cosine_table, sine_table):
    half_dim = values.shape[-1] // 2
    first_half = values[..., :half_dim]
    second = values[..., half_dim:]
    cos_part = cosine_table[:, None, :]
    sin_part = sine_table[:, None, :]
    return jnp.concatenate(
        [first_half * cos_part - second * sin_part, second * cos_part + first_half * sin_part],
        axis=-1,
    )


def inverse_rotation(values, cosine_table, sine_table):
    half_dim = values.shape[-1] // 2
    first_half = values[..., :half_dim]
    second = values[..., half_dim:]
    cos_part = cosine_table[:, None, :]
    sin_part = sine_table[:, None, :]
    return jnp.concatenate(
        [first_half * cos_part + second * sin_part, second * cos_part - first_half * sin_part],
        axis=-1,
    )


def swap(value, axis, bit, size):
    return lax.ppermute(value, axis, [(i, i ^ bit) for i in range(size)])


def gather_steps(value, steps, sizes, places):
    held, done = value, []
    for axis, bit in steps:
        got = swap(held, axis, bit, sizes[axis])
        upper = (places[axis] & bit) != 0
        at = len([d for d in done if (d[0] == "dp" and axis == "group") or (d[0] == axis and d[1] > bit)])
        low_part, high_part = jnp.where(upper, got, held), jnp.where(upper, held, got)
        inner = held.shape[at:]
        flat = held.shape[:at] + (-1,) + value.shape[1:]
        low_part, high_part = low_part.reshape(flat), high_part.reshape(flat)
        held = jnp.concatenate([low_part, high_part], axis=at)
        held = held.reshape(held.shape[:at] + (2,) + inner)
        done = done + [(axis, bit)]
    return held


class Chain:
    def __init__(self, held, steps, done, sizes, places):
        self.held, self.steps, self.done = held, list(steps), list(done)
        self.sizes, self.places = sizes, places

    def start(self):
        axis, bit = self.steps.pop(0)
        if (axis, bit) in self.done:
            at = self.done.index((axis, bit))
            mine = ((self.places[axis] & bit) != 0).astype(jnp.int32)
            sent = lax.dynamic_index_in_dim(self.held, 1 - mine, at, keepdims=False)
            self.kept = lax.dynamic_index_in_dim(self.held, mine, at, keepdims=False)
            self.done.pop(at)
        else:
            sent = self.kept = self.held
        return swap(sent, axis, bit, self.sizes[axis])

    def finish(self, got):
        self.total = self.kept.astype(jnp.float32) + got.astype(jnp.float32)
        self.held = self.total.astype(jnp.bfloat16)


class TokenChain(Chain):
    def start(self):
        axis, bit = self.steps.pop(0)
        half = self.held.shape[0] // 2
        self.kept = self.held[:half]
        return swap(self.held[half:], axis, bit, self.sizes[axis])


def start_all(chains):
    return tuple(chain.start() for chain in chains)


def finish_all(chains, gots, behind=()):
    gots = lax.optimization_barrier(tuple(gots) + tuple(behind))[: len(gots)]
    for chain, got in zip(chains, gots):
        chain.finish(got)
    return gots


def dot(left_op, right_op, left_dim, right_dim):
    return lax.dot_general(
        left_op, right_op, (((left_dim,), (right_dim,)), ((), ())), preferred_element_type=jnp.float32
    )


def mix_kernel(normed_ref, cot_ref, gate_ref, up_ref, down_ref, kept_ref, sent_ref, hidden_ref, dg_ref, du_ref):
    normed = normed_ref[...]
    gate_value = dot(normed, gate_ref[...], 1, 1)
    up_value = dot(normed, up_ref[...], 1, 1)
    d_hidden = dot(cot_ref[...], down_ref[...], 1, 0)
    sigmoid_gate = jax.nn.sigmoid(gate_value)
    silu_gate = gate_value * sigmoid_gate
    hidden_ref[...] = (silu_gate * up_value).astype(jnp.bfloat16)
    d_gate = (
        d_hidden * up_value * sigmoid_gate * (1.0 + gate_value * (1.0 - sigmoid_gate))
    ).astype(jnp.bfloat16)
    d_up = (d_hidden * silu_gate).astype(jnp.bfloat16)
    dg_ref[...] = d_gate
    du_ref[...] = d_up
    d_normed = dot(d_gate, gate_ref[...], 1, 0) + dot(d_up, up_ref[...], 1, 0)

    @pl.when(pl.program_id(0) == 0)
    def _():
        kept_ref[...] = d_normed.astype(jnp.bfloat16)

    @pl.when(pl.program_id(0) == 1)
    def _():
        sent_ref[...] = d_normed.astype(jnp.bfloat16)


def feed_forward(normed, cot, w_gate_t, w_up_t, w_down_t):
    count, width = normed.shape
    units = w_gate_t.shape[0]
    step = count // 2
    whole = lambda shape: pl.BlockSpec(shape, lambda i: (0, 0))
    rows = lambda cols: pl.BlockSpec((step, cols), lambda i: (i, 0))
    shape = lambda cols: jax.ShapeDtypeStruct((count, cols), jnp.bfloat16)
    return pl.pallas_call(
        mix_kernel,
        grid=(2,),
        in_specs=[
            rows(width),
            rows(width),
            whole((units, width)),
            whole((units, width)),
            whole((width, units)),
        ],
        out_specs=[whole((step, width)), whole((step, width)), rows(units), rows(units), rows(units)],
        out_shape=[jax.ShapeDtypeStruct((step, width), jnp.bfloat16)] * 2
        + [shape(units), shape(units), shape(units)],
        compiler_params=pltpu.CompilerParams(vmem_limit_bytes=56 << 20),
        cost_estimate=pl.CostEstimate(
            flops=10 * count * units * width, transcendentals=count * units, bytes_accessed=12 << 20
        ),
        name="feed_forward",
    )(normed, cot, w_gate_t, w_up_t, w_down_t)


def grad_kernel(normed_ref, cot_ref, hidden_ref, dg_ref, du_ref, pair_ref, down_ref):
    pair_ref[0] = dot(dg_ref[...], normed_ref[...], 0, 0).astype(jnp.bfloat16)
    pair_ref[1] = dot(du_ref[...], normed_ref[...], 0, 0).astype(jnp.bfloat16)
    down_ref[...] = dot(cot_ref[...], hidden_ref[...], 0, 0).astype(jnp.bfloat16)


def feed_forward_grads(normed, cot, hidden, d_gate, d_up):
    count, width = normed.shape
    units = hidden.shape[1]
    vmem = pl.BlockSpec(memory_space=pltpu.VMEM)
    return pl.pallas_call(
        grad_kernel,
        in_specs=[vmem] * 5,
        out_specs=[vmem] * 2,
        out_shape=[
            jax.ShapeDtypeStruct((2, units, width), jnp.bfloat16),
            jax.ShapeDtypeStruct((width, units), jnp.bfloat16),
        ],
        compiler_params=pltpu.CompilerParams(vmem_limit_bytes=56 << 20),
        cost_estimate=pl.CostEstimate(
            flops=6 * count * units * width, transcendentals=0, bytes_accessed=8 << 20
        ),
        name="feed_forward_grads",
    )(normed, cot, hidden, d_gate, d_up)


def row_major(value):
    return with_layout_constraint(value, Layout(major_to_minor=tuple(range(value.ndim))))


def split_features(values, parts):
    width = values.shape[1] // parts
    return jnp.stack([values[:, i * width : (i + 1) * width] for i in range(parts)])


def join_features(blocks):
    return jnp.concatenate([blocks[i] for i in range(blocks.shape[0])], axis=1)


def adam_update(master, mean_old, square_old, gradient, rate, decay):
    momentum = BETA_ONE * mean_old + (1.0 - BETA_ONE) * gradient
    variance = BETA_TWO * square_old + (1.0 - BETA_TWO) * gradient * gradient
    fix_one = 1.0 - BETA_ONE**ADAM_STEP
    fix_two = 1.0 - BETA_TWO**ADAM_STEP
    update = momentum / fix_one / (jnp.sqrt(variance / fix_two) + ADAM_EPS) + decay * master
    return (master - rate * update, momentum, variance)


def per_device(
    tokens,
    cotangent,
    prenorm_master,
    query_master,
    key_master_copy,
    value_master_copy,
    out_master,
    midnorm_master,
    gate_master,
    up_master,
    down_master,
    prenorm_mean,
    query_mean,
    key_first_moment,
    value_first_moment,
    out_mean,
    midnorm_mean,
    gate_mean,
    up_mean,
    down_mean,
    prenorm_square,
    query_square,
    key_second_moment,
    value_second_moment,
    out_square,
    midnorm_square,
    gate_square,
    up_square,
    down_square,
):
    masters = (
        prenorm_master,
        query_master,
        key_master_copy,
        value_master_copy,
        out_master,
        midnorm_master,
        gate_master,
        up_master,
        down_master,
    )
    low = jnp.bfloat16
    n_group, n_dp = lax.axis_size("group"), lax.axis_size("dp")
    my_group, my_dp = lax.axis_index("group"), lax.axis_index("dp")
    group_bits = [1 << i for i in range(n_group.bit_length() - 1)][::-1]
    dp_bits = [1 << i for i in range(n_dp.bit_length() - 1)][::-1]
    sizes = {"dp": n_dp, "group": n_group}
    places = {"dp": my_dp, "group": my_group}
    dp_steps = [("dp", bit) for bit in dp_bits]
    group_steps = [("group", bit) for bit in group_bits]
    far_steps, near_steps = group_steps[:-1], group_steps[-1:]
    wide_first = dp_steps + far_steps + near_steps
    far_first = far_steps + dp_steps + near_steps
    dp_twos, group_twos = (2,) * len(dp_bits), (2,) * len(group_bits)

    def gather_dp(block):
        held = gather_steps(block, dp_steps, sizes, places)
        return held.reshape((n_dp,) + block.shape)

    def gather_group(block):
        held = gather_steps(block, group_steps, sizes, places)
        return held.reshape((n_group,) + block.shape)

    def gather_tokens(block):
        held = block
        for axis, bit in group_steps:
            held = jnp.concatenate([held, swap(held, axis, bit, sizes[axis])], axis=0)
        return held

    def gather_both(block, steps):
        held = gather_steps(block, steps, sizes, places)
        return held.reshape((n_dp, n_group) + block.shape)

    def chain_both(blocks, steps):
        held = blocks.reshape(dp_twos + group_twos + blocks.shape[2:])
        return Chain(held, steps[::-1], dp_steps + group_steps, sizes, places)

    def chain_units(grads, steps):
        held = grads.reshape(dp_twos + (grads.shape[0] // n_dp, grads.shape[1]))
        return Chain(held, steps, dp_steps, sizes, places)

    def chain_tokens(values):
        return TokenChain(values, group_steps[::-1], (), sizes, places)

    rows = tokens.shape[0]
    width = tokens.shape[1]
    part = width // n_group
    gains = jnp.stack([prenorm_master, midnorm_master]).astype(low)
    gains_all = join_features(gather_group(gains)).astype(jnp.float32)
    gain_first, gain_second = gains_all[0:1], gains_all[1:2]

    query_block = query_master.astype(low).T
    kv_block = jnp.concatenate([key_master_copy.astype(low).T, value_master_copy.astype(low).T], axis=0)
    k_cols = key_master_copy.shape[1]
    w_query_t = gather_both(query_block, wide_first).swapaxes(0, 1).reshape(n_group, width, part)
    kv_blocks = gather_both(kv_block, far_first).swapaxes(0, 1)
    w_kv_t = jnp.concatenate(
        [
            kv_blocks[:, :, :k_cols].reshape(n_group, n_dp * k_cols, part),
            kv_blocks[:, :, k_cols:].reshape(n_group, n_dp * k_cols, part),
        ],
        axis=1,
    )
    w_out_t = gather_both(out_master.astype(low).T, wide_first).swapaxes(0, 1)
    w_out_t = w_out_t.reshape(n_group, width, part)

    unit = gate_master.shape[1] // n_group
    unit_rows = n_dp // n_group
    down_cols = down_master.shape[1]
    gate_up_block = jnp.concatenate(
        [
            gate_master.astype(low).T.reshape(n_group, unit, part),
            up_master.astype(low).T.reshape(n_group, unit, part),
        ],
        axis=1,
    )
    down_block = down_master.astype(low).reshape(unit_rows, n_group, unit, down_cols)
    down_block = down_block.transpose(1, 0, 2, 3).reshape(n_group, unit_rows * unit, down_cols)
    down_block = down_block.reshape(n_group, 2 * unit, part // 2)
    moved = jnp.concatenate([gate_up_block, down_block], axis=2)
    moved = lax.all_to_all(moved, "group", 0, 0, tiled=True)
    gate_up_block = join_features(moved[:, :, :part])
    down_block = row_major(moved[:, :, part:].reshape(n_dp * unit, down_cols).T)
    w_gate_t = gather_dp(gate_up_block[:unit]).reshape(n_dp * unit, width)
    w_up_t = gather_dp(gate_up_block[unit:]).reshape(n_dp * unit, width)
    w_down_t = gather_dp(down_block).reshape(width, n_dp * unit)

    cot_held = gather_tokens(cotangent)

    sequence_count = rows // SEQUENCE_LENGTH
    heads_per_group = QUERY_HEADS // KEY_VALUE_HEADS
    score_scale = HEAD_SIZE ** (-0.5)
    q_width = QUERY_HEADS * HEAD_SIZE
    k_width = KEY_VALUE_HEADS * HEAD_SIZE
    tok_float = tokens.astype(jnp.float32)
    inv_one = lax.rsqrt(jnp.mean(tok_float * tok_float, axis=-1, keepdims=True) + EPS_NORM)
    scaled_one = tok_float * inv_one
    normed_one = (scaled_one * gain_first).astype(low)
    normed_rel = split_features(normed_one, n_group)

    def project(blocks, weights):
        total = dot(blocks[0], weights[0], 1, 1)
        for r in range(1, n_group):
            total = total + dot(blocks[r], weights[r], 1, 1)
        return total

    query_raw = project(normed_rel, w_query_t)
    kv_raw = project(normed_rel, w_kv_t)
    key_unrotated, value_projected = kv_raw[:, :k_width], kv_raw[:, k_width:]
    cosine_table, sine_table = rotary_tables(SEQUENCE_LENGTH, HEAD_SIZE)
    query_rotated = apply_rotation(
        query_raw.reshape(sequence_count, SEQUENCE_LENGTH, QUERY_HEADS, HEAD_SIZE),
        cosine_table,
        sine_table,
    ).astype(low)
    query_grouped = query_rotated.reshape(
        sequence_count, SEQUENCE_LENGTH, KEY_VALUE_HEADS, heads_per_group, HEAD_SIZE
    )
    key_rotated = apply_rotation(
        key_unrotated.reshape(sequence_count, SEQUENCE_LENGTH, KEY_VALUE_HEADS, HEAD_SIZE),
        cosine_table,
        sine_table,
    ).astype(low)
    value_reduced = value_projected.reshape(
        sequence_count, SEQUENCE_LENGTH, KEY_VALUE_HEADS, HEAD_SIZE
    ).astype(low)
    scores = weighted_values("sqkgd,spkd->skgqp", query_grouped, key_rotated) * score_scale
    causal = jnp.arange(SEQUENCE_LENGTH)[:, None] >= jnp.arange(SEQUENCE_LENGTH)[None, :]
    raw_weights = jnp.where(causal, jnp.exp(scores), 0.0)
    prob_full = raw_weights / jnp.sum(raw_weights, axis=-1, keepdims=True)
    probability_reduced = prob_full.astype(low)
    attended = weighted_values("skgqp,spkd->sqkgd", probability_reduced, value_reduced)
    attended_low = attended.reshape(rows, q_width).astype(low)
    attended_rel = split_features(attended_low, n_group)
    middle = tok_float + project(attended_rel, w_out_t)
    inv_two = lax.rsqrt(jnp.mean(middle * middle, axis=-1, keepdims=True) + EPS_NORM)
    scaled_two = middle * inv_two
    normed_two = (scaled_two * gain_second).astype(low)
    normed_all = gather_tokens(normed_two)
    d_normed_kept, d_normed_sent, hidden, d_gate, d_up = feed_forward(
        normed_all, cot_held, w_gate_t, w_up_t, w_down_t
    )
    mid = TokenChain(None, group_steps[::-1], (), sizes, places)
    axis, bit = mid.steps.pop(0)
    mid.kept = d_normed_kept
    got = swap(d_normed_sent, axis, bit, sizes[axis])
    hidden, d_gate, d_up, got = lax.optimization_barrier((hidden, d_gate, d_up, got))
    mid.finish(got)
    got = mid.start()
    pair_grad, down_grad = feed_forward_grads(normed_all, cot_held, hidden, d_gate, d_up)
    ffn = [
        Chain(
            pair_grad.reshape((2,) + dp_twos + (unit, width)),
            dp_steps[::-1],
            [("pair", 0)] + dp_steps,
            sizes,
            places,
        ),
        chain_units(down_grad, dp_steps[-2:-1] + dp_steps[:-2] + dp_steps[-1:]),
    ]
    mid.finish(got)
    d_normed_two = mid.total

    cot_float = cotangent.astype(jnp.float32)
    midnorm_sum = jnp.sum(d_normed_two * scaled_two, axis=0, keepdims=True)
    d_scaled_two = d_normed_two * gain_second
    d_middle = cot_float + inv_two * (
        d_scaled_two - scaled_two * jnp.mean(d_scaled_two * scaled_two, axis=-1, keepdims=True)
    )
    d_middle_low = d_middle.astype(low)

    def weight_grad(columns, blocks):
        return jnp.stack([dot(columns, blocks[r], 0, 0).astype(low) for r in range(n_group)])

    def input_part(columns, weights):
        return jnp.stack([dot(columns, weights[r], 1, 0) for r in range(n_group)])

    def by_owner(grads, columns):
        return grads.reshape(n_group, n_dp, columns, part).swapaxes(0, 1)

    out_chain = chain_both(
        by_owner(weight_grad(d_middle_low, attended_rel), width // n_dp), wide_first
    )
    out_got = out_chain.start()
    attended_gradient = join_features(input_part(d_middle_low, w_out_t).astype(low))
    attended_gradient = attended_gradient.reshape(
        sequence_count, SEQUENCE_LENGTH, KEY_VALUE_HEADS, heads_per_group, HEAD_SIZE
    )
    attended_gradient, out_got = lax.optimization_barrier((attended_gradient, out_got))
    out_chain.finish(out_got)
    out_ahead = out_chain.start()
    d_prob = weighted_values("sqkgd,spkd->skgqp", attended_gradient, value_reduced)
    inner_sum = jnp.sum(prob_full * d_prob, axis=-1, keepdims=True)
    d_score = (prob_full * (d_prob - inner_sum) * score_scale).astype(low)
    d_query = weighted_values("skgqp,spkd->sqkgd", d_score, key_rotated).reshape(
        sequence_count, SEQUENCE_LENGTH, QUERY_HEADS, HEAD_SIZE
    )
    d_query = inverse_rotation(d_query, cosine_table, sine_table).reshape(rows, q_width).astype(low)
    key_gradient = weighted_values("fceti,ftcel->ficl", d_score, query_grouped)
    key_gradient = (
        inverse_rotation(key_gradient, cosine_table, sine_table).reshape(rows, k_width).astype(low)
    )
    value_gradient = (
        weighted_values("fceti,ftcel->ficl", probability_reduced, attended_gradient)
        .reshape(rows, k_width)
        .astype(low)
    )
    kv_gradient = jnp.concatenate([key_gradient, value_gradient], axis=1)
    d_normed_blocks = input_part(d_query, w_query_t) + input_part(kv_gradient, w_kv_t)
    d_normed_one = join_features(d_normed_blocks)
    prenorm_sum = jnp.sum(d_normed_one * scaled_one, axis=0, keepdims=True)
    d_scaled_one = d_normed_one * gain_first
    input_grad = d_middle + inv_one * (
        d_scaled_one - scaled_one * jnp.mean(d_scaled_one * scaled_one, axis=-1, keepdims=True)
    )
    gain_rows = jnp.concatenate([prenorm_sum, midnorm_sum], axis=0)

    query_chain = chain_both(by_owner(weight_grad(d_query, normed_rel), q_width // n_dp), wide_first)
    kv_sum = jnp.concatenate(
        [
            by_owner(weight_grad(key_gradient, normed_rel), k_cols),
            by_owner(weight_grad(value_gradient, normed_rel), k_cols),
        ],
        axis=2,
    )
    kv_chain = chain_both(kv_sum, far_first)
    gain_held = split_features(gain_rows, n_group).astype(low).reshape(group_twos + (2, part))
    gain_chain = Chain(gain_held, group_steps[::-1] + dp_steps, group_steps, sizes, places)
    hidden_late, _ = lax.optimization_barrier((hidden, d_score))
    out_part = dot(hidden_late, w_down_t, 1, 1)
    token_chain = chain_tokens(out_part.astype(low))
    pace = [query_chain, kv_chain, out_chain, gain_chain, token_chain]
    pending = start_all(ffn)
    count = 0
    while any(chain.steps for chain in pace):
        live = [chain for chain in pace if chain.steps or (count == 0 and chain is out_chain)]
        gots = [
            out_ahead if count == 0 and chain is out_chain else chain.start() for chain in live
        ]
        gots = finish_all(live, gots)
        if count != 2 or not any(chain.steps for chain in pace):
            while pending:
                finish_all(ffn, pending, gots[:1])
                pending = start_all(ffn) if ffn[0].steps else ()
                if any(chain.steps for chain in pace):
                    break
        count += 1
    query_own = row_major(row_major(query_chain.total).T)
    out_own = row_major(row_major(out_chain.total).T)
    kv_own = kv_chain.total
    key_own, value_own = kv_own[:k_cols].T, kv_own[k_cols:].T
    prenorm_own, midnorm_own = gain_chain.total[0], gain_chain.total[1]
    output = middle + token_chain.total

    gate_up_back = split_features(ffn[0].held.reshape(2 * unit, width), n_group)
    down_back = row_major(ffn[1].held).T.reshape(n_group, unit_rows * unit, down_cols)
    down_back = down_back.reshape(n_group, 2 * unit, part // 2)
    back = jnp.concatenate([gate_up_back, down_back], axis=2)
    back = lax.all_to_all(back, "group", 0, 0, tiled=True)
    gate_own = back[:, :unit, :part].reshape(n_group * unit, part).T.astype(jnp.float32)
    up_own = back[:, unit:, :part].reshape(n_group * unit, part).T.astype(jnp.float32)
    down_back = back[:, :, part:].reshape(n_group, unit_rows, unit, down_cols).transpose(1, 0, 2, 3)
    down_own = down_back.reshape(n_dp * unit, down_cols).astype(jnp.float32)
    down_own = with_layout_constraint(down_own, Layout(major_to_minor=(1, 0)))
    owned = (
        prenorm_own,
        query_own,
        key_own,
        value_own,
        out_own,
        midnorm_own,
        gate_own,
        up_own,
        down_own,
    )
    mean_list = (
        prenorm_mean,
        query_mean,
        key_first_moment,
        value_first_moment,
        out_mean,
        midnorm_mean,
        gate_mean,
        up_mean,
        down_mean,
    )
    square_list = (
        prenorm_square,
        query_square,
        key_second_moment,
        value_second_moment,
        out_square,
        midnorm_square,
        gate_square,
        up_square,
        down_square,
    )
    rate_list = (
        RATE_GAIN,
        RATE_MATRIX,
        RATE_MATRIX,
        RATE_MATRIX,
        RATE_OUTPUT,
        RATE_GAIN,
        RATE_MATRIX,
        RATE_MATRIX,
        RATE_MATRIX,
    )
    decays = (
        0.0,
        DECAY_RATE,
        DECAY_RATE,
        DECAY_RATE,
        DECAY_RATE,
        0.0,
        DECAY_RATE,
        DECAY_RATE,
        DECAY_RATE,
    )
    results = [
        adam_update(masters[k], mean_list[k], square_list[k], owned[k], rate_list[k], decays[k])
        for k in range(9)
    ]
    return (
        output,
        input_grad,
        owned[0],
        owned[1],
        owned[2],
        owned[3],
        owned[4],
        owned[5],
        owned[6],
        owned[7],
        owned[8],
        results[0][0],
        results[1][0],
        results[2][0],
        results[3][0],
        results[4][0],
        results[5][0],
        results[6][0],
        results[7][0],
        results[8][0],
        results[0][1],
        results[1][1],
        results[2][1],
        results[3][1],
        results[4][1],
        results[5][1],
        results[6][1],
        results[7][1],
        results[8][1],
        results[0][2],
        results[1][2],
        results[2][2],
        results[3][2],
        results[4][2],
        results[5][2],
        results[6][2],
        results[7][2],
        results[8][2],
    )


def solution(mesh):
    placed = (
        P(("dp", "group"), None),
        P(("dp", "group"), None),
        P("group"),
        P("group", "dp"),
        P("group", "dp"),
        P("group", "dp"),
        P("group", "dp"),
        P("group"),
        P("group", "dp"),
        P("group", "dp"),
        P("group", "dp"),
        P("group"),
        P("group", "dp"),
        P("group", "dp"),
        P("group", "dp"),
        P("group", "dp"),
        P("group"),
        P("group", "dp"),
        P("group", "dp"),
        P("group", "dp"),
        P("group"),
        P("group", "dp"),
        P("group", "dp"),
        P("group", "dp"),
        P("group", "dp"),
        P("group"),
        P("group", "dp"),
        P("group", "dp"),
        P("group", "dp"),
    )
    return jax.shard_map(
        per_device,
        mesh=mesh,
        in_specs=placed,
        out_specs=(
            P(("dp", "group"), None),
            P(("dp", "group"), None),
            P("group"),
            P("group", "dp"),
            P("group", "dp"),
            P("group", "dp"),
            P("group", "dp"),
            P("group"),
            P("group", "dp"),
            P("group", "dp"),
            P("group", "dp"),
            P("group"),
            P("group", "dp"),
            P("group", "dp"),
            P("group", "dp"),
            P("group", "dp"),
            P("group"),
            P("group", "dp"),
            P("group", "dp"),
            P("group", "dp"),
            P("group"),
            P("group", "dp"),
            P("group", "dp"),
            P("group", "dp"),
            P("group", "dp"),
            P("group"),
            P("group", "dp"),
            P("group", "dp"),
            P("group", "dp"),
            P("group"),
            P("group", "dp"),
            P("group", "dp"),
            P("group", "dp"),
            P("group", "dp"),
            P("group"),
            P("group", "dp"),
            P("group", "dp"),
            P("group", "dp"),
        ),
        check_vma=False,
    )
```
